32 devices in a mesh: dp: 8 (over y, x, core), tensor: 4 (over z).
Axes of the slice: x: 2, y: 2, z: 4, core: 2. Of those that a mesh axis runs over, the one named last changes fastest.
Arguments:
- tokens: bfloat16 [2, 4096, 2048], P(None, ('dp', 'tensor')), may hold values from -6 to 6
- cotangent: bfloat16 [2, 4096, 2048], P(None, ('dp', 'tensor')), may hold values from -6 to 6
- doc_lengths: int32 [2, 8, 2], P(None, 'dp'), may hold values from 1 to 448, as said below
- attn_gain: bfloat16 [2048], P('dp'), may hold values from 0.099609375 to 1.8984375
- w_qkv: bfloat16 [2048, 3, 2048], P('dp', None, 'tensor'), may hold values from -0.125 to 0.125
- w_beta: bfloat16 [2048, 16], P('dp', 'tensor'), may hold values from -0.125 to 0.125
- conv_weight: bfloat16 [3, 4, 16, 128], P(None, None, 'tensor', 'dp'), may hold values from -3 to 3
- head_gain: bfloat16 [128], P('dp'), may hold values from 0.099609375 to 1.8984375
- w_out: bfloat16 [2048, 2048], P('tensor', 'dp'), may hold values from -0.125 to 0.125
- ffn_gain: bfloat16 [2048], P('dp'), may hold values from 0.099609375 to 1.8984375
- w_gate_up: bfloat16 [2048, 2, 5632], P('dp', None, 'tensor'), may hold values from -0.125 to 0.125
- w_down: bfloat16 [5632, 2048], P('tensor', 'dp'), may hold values from -0.125 to 0.125
Outputs:
- layer_out: bfloat16 [2, 4096, 2048], P(None, ('dp', 'tensor'))
- tokens_grad: float32 [2, 4096, 2048], P(None, ('dp', 'tensor'))
- attn_gain_grad: float32 [2048], P('dp')
- w_qkv_grad: float32 [2048, 3, 2048], P('dp', None, 'tensor')
- w_beta_grad: float32 [2048, 16], P('dp', 'tensor')
- conv_weight_grad: float32 [3, 4, 16, 128], P(None, None, 'tensor', 'dp')
- head_gain_grad: float32 [128], P('dp')
- w_out_grad: float32 [2048, 2048], P('tensor', 'dp')
- ffn_gain_grad: float32 [2048], P('dp')
- w_gate_up_grad: float32 [2048, 2, 5632], P('dp', None, 'tensor')
- w_down_grad: float32 [5632, 2048], P('tensor', 'dp')
The draws below stay inside these ranges and needn't reach their ends.
Inputs may be any that keep to these rules, and one draw needn't show every extreme that they name: doc_lengths[m, g] gives the lengths of the two documents packed into buffer g of micro-batch m; each document begins at a multiple of 64 slots, ceil(L1 / 64) + ceil(L2 / 64) is at most 8 and at least half of that, rounded down; the longest reaches the maximum.
All inputs are finite; a program needn't handle non-finite values.
Results may differ from the reference program's by a relative error of at most 0.014.
Values may be sent and summed in bfloat16 or wider, within the bound.
No kernel may reach another device: no remote copies, remote signals or barrier semaphores. Data moves between devices by JAX's collectives and lax.ppermute only.
A program may use at most 320 MiB of HBM per device.

```python
import jax
import jax.numpy as jnp
from jax import lax

D = 2048
H = 16
DH = 128
FF = 5632
BLOCK = 64
MB = 2
TOK_DEV = 128
TOKENS = 4096
N_DP = 8
N_TENSOR = 4


def draw_doc_lengths(key, part):
    block_total = TOK_DEV * N_TENSOR // BLOCK
    key_list = jax.random.split(key, 3)
    used_blocks = jax.random.randint(key_list[0], (MB, N_DP), block_total // 2, block_total + 1)
    used_blocks = used_blocks.at[0, 0].set(block_total)
    first_blocks = jax.random.randint(key_list[1], (MB, N_DP), 1, used_blocks)
    first_blocks = first_blocks.at[0, 0].set(block_total - 1)
    second_blocks = used_blocks - first_blocks
    tail_rows = jax.random.randint(key_list[2], (MB, N_DP, 2), 1, BLOCK + 1)
    tail_rows = tail_rows.at[0, 0, 0].set(BLOCK)
    counts = jnp.stack([first_blocks, second_blocks], -1)
    return (BLOCK * (counts - 1) + tail_rows).astype(jnp.int32)


def levels(own_key, dims, cuts, least, high):
    loudness = 1.0
    for position, parts in cuts:
        steps = jax.random.uniform(jax.random.fold_in(jax.random.fold_in(own_key, 6), position), (parts,), jnp.float32, least / len(cuts), high / len(cuts))
        loudness = loudness * jnp.repeat(jnp.exp(steps), dims[position] // parts).reshape((-1,) + (1,) * (len(dims) - 1 - position))
    return loudness


def scatter_about(rng, shape, width, most, cuts=(), kind=jnp.bfloat16):
    gain = levels(rng, shape, cuts, -0.22, 0.18) if cuts else 1.0
    values = jax.random.normal(rng, shape, jnp.float32) * width * gain
    return jnp.minimum(jnp.maximum(values, -most), most).astype(kind)


def setup_inputs(seed: int = 0) -> dict:
    splits = jax.random.split(jax.random.key(seed), 13)
    tokens = scatter_about(splits[0], (MB, TOKENS, D), 1.0, 6.0, ((1, 32),))
    cotangent = scatter_about(splits[1], (MB, TOKENS, D), 1.0, 6.0, ((1, 32),))
    doc_lengths = draw_doc_lengths(jax.random.fold_in(splits[12], 71), 0)
    attn_gain = jnp.clip(1.0 + 0.18 * jax.random.normal(splits[3], (D,), jnp.float32), 0.099609375, 1.8984375).astype(jnp.bfloat16)
    w_qkv = scatter_about(splits[4], (D, 3, D), D ** -0.5, 0.125, ((0, 8), (2, 4)))
    w_beta = scatter_about(splits[5], (D, H), D ** -0.5, 0.125, ((0, 8), (1, 4)))
    conv_weight = scatter_about(splits[6], (3, 4, H, DH), 4 ** -0.5, 3.0, ((2, 4), (3, 8)))
    head_gain = jnp.clip(1.0 + 0.18 * jax.random.normal(splits[7], (DH,), jnp.float32), 0.099609375, 1.8984375).astype(jnp.bfloat16)
    w_out = scatter_about(splits[8], (D, D), D ** -0.5, 0.125, ((0, 4), (1, 8)))
    ffn_gain = jnp.clip(1.0 + 0.18 * jax.random.normal(splits[9], (D,), jnp.float32), 0.099609375, 1.8984375).astype(jnp.bfloat16)
    w_gate_up = scatter_about(splits[10], (D, 2, FF), D ** -0.5, 0.125, ((0, 8), (2, 4)))
    w_down = scatter_about(splits[11], (FF, D), (FF // 3) ** -0.5, 0.125, ((0, 4), (1, 8)))
    return {"tokens": tokens, "cotangent": cotangent, "doc_lengths": doc_lengths, "attn_gain": attn_gain, "w_qkv": w_qkv, "w_beta": w_beta, "conv_weight": conv_weight, "head_gain": head_gain, "w_out": w_out, "ffn_gain": ffn_gain, "w_gate_up": w_gate_up, "w_down": w_down}


NORM_EPS = 1e-06
HEAD_EPS = 1e-05
HIGHEST = lax.Precision.HIGHEST

@jax.custom_vjp
def low(v):
    return lax.optimization_barrier(v.astype(jnp.bfloat16)).astype(jnp.float32)

@jax.custom_vjp
def low_back(v):
    return v

def low_keep(v):
    return (low(v), None)

def low_pass(kept, grad):
    return (grad,)

def back_keep(v):
    return (v, None)

def back_low(kept, grad):
    return (low(grad),)
low.defvjp(low_keep, low_pass)
low_back.defvjp(back_keep, back_low)

def doc_layout(length_pair, slot_count):
    doc_len = length_pair.astype(jnp.int32)
    first_end = (doc_len[0] + BLOCK - 1) // BLOCK * BLOCK
    second_end = first_end + (doc_len[1] + BLOCK - 1) // BLOCK * BLOCK
    places = jnp.arange(slot_count, dtype=jnp.int32)
    in_first = places < first_end
    in_second = jnp.logical_and(places >= first_end, places < second_end)
    doc_begin = jnp.where(in_first, 0, jnp.where(in_second, first_end, second_end))
    doc_limit = jnp.where(in_first, doc_len[0], jnp.where(in_second, doc_len[1], 0))
    offset = places - doc_begin
    is_valid = (offset < doc_limit).astype(jnp.float32)
    return (offset, is_valid)

def rms_scale(values, gain_row):
    return values * lax.rsqrt(lax.optimization_barrier(jnp.mean(values * values, -1, keepdims=True)) + NORM_EPS) * gain_row

def conv_silu(projected, conv_weight, offset):
    slot_count = projected.shape[0]
    channel_count = projected.shape[2]
    conv_taps = jnp.transpose(conv_weight.reshape(3, 4, channel_count), (1, 0, 2))
    convolved = conv_taps[0] * projected
    for lag_step in range(1, 4):
        delayed = jnp.pad(projected[:slot_count - lag_step], ((lag_step, 0), (0, 0), (0, 0)))
        reach_ok = (offset >= lag_step).astype(projected.dtype)[:, None, None]
        convolved = convolved + conv_taps[lag_step] * delayed * reach_ok
    return jax.nn.silu(convolved)

def split_heads(convolved, beta_logit, head_dim, is_valid):
    slot_count = convolved.shape[0]
    head_count = beta_logit.shape[1]
    queries = convolved[:, 0].reshape(slot_count, head_count, head_dim)
    keys_all = convolved[:, 1].reshape(slot_count, head_count, head_dim)
    values_all = convolved[:, 2].reshape(slot_count, head_count, head_dim)
    queries = queries * lax.rsqrt(lax.optimization_barrier(jnp.sum(queries * queries, -1, keepdims=True)) + NORM_EPS) * head_dim ** (-0.5)
    keys_all = keys_all * lax.rsqrt(lax.optimization_barrier(jnp.sum(keys_all * keys_all, -1, keepdims=True)) + NORM_EPS)
    strength = jax.nn.sigmoid(beta_logit) * is_valid[:, None]
    return (queries, keys_all, values_all, strength)

def head_norm(recalls, head_gain, is_valid):
    slot_count = recalls.shape[0]
    normed = recalls * lax.rsqrt(lax.optimization_barrier(jnp.mean(recalls * recalls, -1, keepdims=True)) + HEAD_EPS) * head_gain
    normed = normed * is_valid[:, None, None]
    return normed.reshape(slot_count, recalls.shape[1] * recalls.shape[2])

def token_step(memory, token_item):
    q_tok, k_tok, v_tok, b_tok = token_item
    recall = jnp.einsum('hvk,hk->hv', memory, k_tok, precision=HIGHEST)
    memory = memory + b_tok[:, None, None] * (v_tok - recall)[:, :, None] * k_tok[:, None, :]
    return (memory, jnp.einsum('hvk,hk->hv', memory, q_tok, precision=HIGHEST))

def block_run(memory, inputs):
    memory = memory * (1.0 - inputs[4])
    return lax.scan(token_step, memory, (inputs[0], inputs[1], inputs[2], inputs[3]))

def mixer_reference(projected, beta_logit, conv_weight, head_gain, offset, is_valid):
    slot_count = projected.shape[0]
    head_dim = head_gain.shape[0]
    head_count = beta_logit.shape[1]
    convolved = conv_silu(projected, conv_weight, offset)
    queries, keys_all, values_all, strength = split_heads(convolved, beta_logit, head_dim, is_valid)
    block_count = slot_count // BLOCK

    def blocked(tensor):
        return tensor.reshape((block_count, BLOCK) + tensor.shape[1:])
    restart = (offset.reshape(block_count, BLOCK)[:, 0] == 0).astype(projected.dtype)
    initial = jnp.zeros((head_count, head_dim, head_dim), projected.dtype)
    final_state, recalls = lax.scan(jax.checkpoint(block_run), initial, (blocked(queries), blocked(keys_all), blocked(values_all), blocked(strength), restart))
    recalls = recalls.reshape(slot_count, head_count, head_dim)
    return head_norm(recalls, head_gain, is_valid)

def layer(row_values, params, offset, is_valid):
    attn_gain, w_qkv, w_beta, conv_weight, head_gain, w_out, ffn_gain, w_gate_up, w_down = params
    group_slots = row_values.shape[0]
    model_width = row_values.shape[1]
    unit_count = w_down.shape[0]
    attn_in = low(rms_scale(row_values, attn_gain))
    projected = low_back(jnp.dot(attn_in, w_qkv.reshape(model_width, 3 * model_width), precision=HIGHEST))
    projected = projected.reshape(group_slots, 3, model_width)
    beta_logit = low_back(jnp.dot(attn_in, w_beta, precision=HIGHEST))
    mixed = low(mixer_reference(projected, beta_logit, conv_weight, head_gain, offset, is_valid))
    branch = low_back(jnp.dot(mixed, w_out, precision=HIGHEST))
    hidden = row_values + branch
    ffn_in = low(rms_scale(hidden, ffn_gain))
    gate_up = low_back(jnp.dot(ffn_in, w_gate_up.reshape(model_width, 2 * unit_count), precision=HIGHEST))
    gate_up = gate_up.reshape(group_slots, 2, unit_count)
    activated = low(jax.nn.silu(gate_up[:, 0]) * gate_up[:, 1])
    return hidden + jnp.dot(activated, w_down, precision=HIGHEST)

def reference(tokens, cotangent, doc_lengths, attn_gain, w_qkv, w_beta, conv_weight, head_gain, w_out, ffn_gain, w_gate_up, w_down):
    group_slots = TOK_DEV * N_TENSOR
    batches = tokens.shape[0]
    group_count = tokens.shape[1] // group_slots
    model_width = tokens.shape[2]
    token_f = tokens.astype(jnp.float32).reshape(batches * group_count, group_slots, model_width)
    cot_f = cotangent.astype(jnp.float32).reshape(batches * group_count, group_slots, model_width)
    length_pairs = doc_lengths.reshape(batches * group_count, 2)
    weight_set = tuple((weight_item.astype(jnp.float32) for weight_item in (attn_gain, w_qkv, w_beta, conv_weight, head_gain, w_out, ffn_gain, w_gate_up, w_down)))
    zero_grads = tuple((jnp.zeros_like(weight_item) for weight_item in weight_set))

    def per_group(totals, items):
        group_rows, group_cot, length_pair = items
        offset, is_valid = doc_layout(length_pair, group_slots)

        def forward(row_values, *params):
            return layer(row_values, params, offset, is_valid)
        result, pullback = jax.vjp(forward, group_rows, *weight_set)
        gradients = pullback(group_cot)
        totals = tuple((total_item + grad_item for total_item, grad_item in zip(totals, gradients[1:])))
        return (totals, (result.astype(jnp.bfloat16), gradients[0]))
    totals, (layer_rows, input_rows) = lax.scan(per_group, zero_grads, (token_f, cot_f, length_pairs))
    return (layer_rows.reshape(tokens.shape), input_rows.reshape(tokens.shape), totals[0], totals[1], totals[2], totals[3], totals[4], totals[5], totals[6], totals[7], totals[8])
```

```python
import jax
import jax.numpy as jnp
from jax import lax
from jax.experimental import pallas as pl
from jax.experimental.pallas import tpu as pltpu
from jax.sharding import PartitionSpec as P

BLOCK = 64
NORM_EPS = 1e-06
HEAD_EPS = 1e-05
F32 = jnp.float32
BF16 = jnp.bfloat16
LANES = 128
HALO = 8


def low_dot(left, right, left_dim, right_dim):
    return lax.dot_general(
        left.astype(BF16),
        right.astype(BF16),
        (((left_dim,), (right_dim,)), ((), ())),
        preferred_element_type=F32,
    )


def sigmoid(value):
    return 1.0 / (1.0 + jnp.exp(-value))


def block_masks(rows):
    row = lax.broadcasted_iota(jnp.int32, (rows, rows), 0)
    col = lax.broadcasted_iota(jnp.int32, (rows, rows), 1)
    same = {size: (row // size) == (col // size) for size in (8, 16, 32, 64)}
    strict = jnp.logical_and(same[64], col < row)
    lower = jnp.logical_and(same[64], col <= row)
    eye = (row == col).astype(F32)
    return same, strict, lower, eye


def unit_inverse(system, same, eye):
    base = jnp.where(same[8], system, 0.0)
    square = low_dot(base, base, 1, 0)
    fourth = low_dot(square, square, 1, 0)
    inverse = eye - base
    inverse = inverse + low_dot(inverse, square, 1, 0)
    inverse = inverse + low_dot(inverse, fourth, 1, 0)
    for size in (8, 16, 32):
        off = jnp.where(jnp.logical_and(same[2 * size], jnp.logical_not(same[size])), system, 0.0)
        inverse = inverse - low_dot(inverse, low_dot(off, inverse, 1, 0), 1, 0)
    return inverse


def delayed_rows(previous, current, lag):
    if lag == 0:
        return current
    rows = current.shape[0]
    joined = jnp.concatenate([previous, current], axis=0)
    return joined[HALO - lag : HALO - lag + rows]


def conv_part(proj_ref, before_ref, conv_ref, reach, part, head, head_dim, heads):
    width = heads * head_dim
    column = part * width + head * head_dim
    current = proj_ref[:, column : column + head_dim]
    previous = before_ref[:, column : column + head_dim]
    taps = [conv_ref[part * 4 + lag : part * 4 + lag + 1, head * head_dim : (head + 1) * head_dim] for lag in range(4)]
    shifted = [current]
    for lag in range(1, 4):
        shifted.append(delayed_rows(previous, current, lag) * reach[lag])
    total = taps[0] * shifted[0]
    for lag in range(1, 4):
        total = total + taps[lag] * shifted[lag]
    return total, shifted, taps


def stack_heads(pieces, index):
    return jnp.concatenate([piece[index * BLOCK : (index + 1) * BLOCK] for piece in pieces], axis=0)


def forward_kernel(
    proj_ref, before_ref, logit_ref, pos_ref, valid_ref, conv_ref, gain_ref,
    mixed_ref, recall_ref, start_ref, inverse_ref, update_ref, weight_ref,
    state_ref, *, heads, head_dim,
):
    rows = proj_ref.shape[0]
    blocks = rows // BLOCK
    stacked = heads * BLOCK

    @pl.when(pl.program_id(0) == 0)
    def _():
        state_ref[...] = jnp.zeros_like(state_ref)

    pos = pos_ref[...]
    valid = valid_ref[...]
    reach = [None] + [(pos >= lag).astype(F32) for lag in range(1, 4)]
    parts = [[], [], []]
    strengths = []
    for head in range(heads):
        for part in range(3):
            total, _, _ = conv_part(proj_ref, before_ref, conv_ref, reach, part, head, head_dim, heads)
            value = total * sigmoid(total)
            if part < 2:
                scale = lax.rsqrt(jnp.sum(value * value, -1, keepdims=True) + NORM_EPS)
                if part == 0:
                    scale = scale * head_dim ** (-0.5)
                value = value * scale
            parts[part].append(value)
        strengths.append(sigmoid(logit_ref[:, head : head + 1]) * valid)
    same, strict, lower, eye = block_masks(stacked)
    local = []
    for index in range(blocks):
        queries = stack_heads(parts[0], index).astype(BF16)
        keys = stack_heads(parts[1], index)
        values = stack_heads(parts[2], index)
        strength = stack_heads(strengths, index)
        keys_low = keys.astype(BF16)
        gram = low_dot(keys_low, keys_low, 1, 1)
        system = jnp.where(strict, strength * gram, 0.0)
        inverse = unit_inverse(system, same, eye).astype(BF16)
        weighted = low_dot(inverse, strength * keys, 1, 0).astype(BF16)
        fresh = low_dot(inverse, strength * values, 1, 0)
        scores = jnp.where(lower, low_dot(queries, keys_low, 1, 1), 0.0).astype(BF16)
        inverse_ref[index] = inverse
        weight_ref[index] = weighted
        local.append((queries, keys_low, weighted, fresh, scores))
    for index in range(blocks):
        queries, keys_low, weighted, fresh, scores = local[index]
        keep = (pos[index * BLOCK : index * BLOCK + 1] != 0).astype(F32)
        updates = []
        carried = []
        for head in range(heads):
            span = slice(head * BLOCK, (head + 1) * BLOCK)
            state = state_ref[head] * keep
            state_low = state.astype(BF16)
            start_ref[index, head] = state_low
            update = fresh[span] - low_dot(weighted[span], state_low, 1, 1)
            update_low = update.astype(BF16)
            updates.append(update_low)
            carried.append(low_dot(queries[span], state_low, 1, 1))
            state_ref[head] = state + low_dot(update_low, keys_low[span], 0, 0)
        update_all = jnp.concatenate(updates, axis=0)
        update_ref[index] = update_all
        recall_all = jnp.concatenate(carried, axis=0) + low_dot(scores, update_all, 1, 0)
        scale = lax.rsqrt(jnp.mean(recall_all * recall_all, -1, keepdims=True) + HEAD_EPS)
        normed = recall_all * scale * gain_ref[...]
        here = slice(index * BLOCK, (index + 1) * BLOCK)
        for head in range(heads):
            span = slice(head * BLOCK, (head + 1) * BLOCK)
            column = slice(head * head_dim, (head + 1) * head_dim)
            recall_ref[here, column] = recall_all[span]
            mixed_ref[here, column] = (normed[span] * valid[here]).astype(BF16)


def backward_kernel(
    proj_ref, before_ref, logit_ref, pos_ref, after_ref, valid_ref, conv_ref, gain_ref,
    recall_ref, start_ref, inverse_ref, update_ref, weight_ref, mixed_grad_ref,
    proj_grad_ref, conv_grad_ref, gain_grad_ref,
    state_ref, halo_ref, *, heads, head_dim,
):
    rows = proj_ref.shape[0]
    blocks = rows // BLOCK
    stacked = heads * BLOCK
    width = heads * head_dim

    @pl.when(pl.program_id(0) == 0)
    def _():
        state_ref[...] = jnp.zeros_like(state_ref)
        halo_ref[...] = jnp.zeros_like(halo_ref)
        conv_grad_ref[...] = jnp.zeros_like(conv_grad_ref)
        gain_grad_ref[...] = jnp.zeros_like(gain_grad_ref)

    pos = pos_ref[...]
    valid = valid_ref[...]
    reach = [None] + [(pos >= lag).astype(F32) for lag in range(1, 4)]
    pos_ahead = jnp.concatenate([pos, after_ref[...]], axis=0)
    reach_ahead = [None] + [(pos_ahead >= lag).astype(F32) for lag in range(1, 4)]
    gain = gain_ref[...]
    parts = [[], [], []]
    gates = []
    recall_grads = []
    gain_grad = jnp.zeros((1, head_dim), F32)
    for head in range(heads):
        for part in range(3):
            total, _, _ = conv_part(proj_ref, before_ref, conv_ref, reach, part, head, head_dim, heads)
            value = total * sigmoid(total)
            if part < 2:
                scale = lax.rsqrt(jnp.sum(value * value, -1, keepdims=True) + NORM_EPS)
                if part == 0:
                    scale = scale * head_dim ** (-0.5)
                value = value * scale
            parts[part].append(value)
        gates.append(sigmoid(logit_ref[:, head : head + 1]))
        column = slice(head * head_dim, (head + 1) * head_dim)
        recall = recall_ref[:, column]
        pulled = mixed_grad_ref[:, column] * valid
        scale = lax.rsqrt(jnp.mean(recall * recall, -1, keepdims=True) + HEAD_EPS)
        normed = recall * scale
        gain_grad = gain_grad + jnp.sum(pulled * normed, 0, keepdims=True)
        pulled = pulled * gain
        recall_grads.append(
            scale * (pulled - normed * jnp.mean(normed * pulled, -1, keepdims=True))
        )
    gain_grad_ref[...] += gain_grad
    strengths = [gate * valid for gate in gates]
    same, strict, lower, eye = block_masks(stacked)
    query_grads = [None] * blocks
    key_grads = [None] * blocks
    value_grads = [None] * blocks
    strength_grads = [None] * blocks
    for index in range(blocks - 1, -1, -1):
        queries = stack_heads(parts[0], index).astype(BF16)
        keys = stack_heads(parts[1], index).astype(BF16)
        values = stack_heads(parts[2], index)
        strength = stack_heads(strengths, index)
        out_grad = stack_heads(recall_grads, index).astype(BF16)
        inverse = inverse_ref[index]
        weighted = weight_ref[index]
        update = update_ref[index]
        gram = low_dot(keys, keys, 1, 1)
        scores = jnp.where(lower, low_dot(queries, keys, 1, 1), 0.0).astype(BF16)
        local_grad = low_dot(scores, out_grad, 0, 0)
        score_grad = jnp.where(lower, low_dot(out_grad, update, 1, 1), 0.0).astype(BF16)
        keep = (pos[index * BLOCK : index * BLOCK + 1] != 0).astype(F32)
        update_grads = []
        query_carried = []
        key_carried = []
        misses = []
        starts = []
        for head in range(heads):
            span = slice(head * BLOCK, (head + 1) * BLOCK)
            ahead = state_ref[head]
            ahead_low = ahead.astype(BF16)
            start = start_ref[index, head]
            starts.append(start)
            update_grad = local_grad[span] + low_dot(keys[span], ahead_low, 1, 1)
            update_grad_low = update_grad.astype(BF16)
            update_grads.append(update_grad_low)
            carried = ahead + low_dot(out_grad[span], queries[span], 0, 0)
            carried = carried - low_dot(update_grad_low, weighted[span], 0, 0)
            state_ref[head] = carried * keep
            query_carried.append(low_dot(out_grad[span], start, 1, 0))
            key_carried.append(low_dot(update[span], ahead_low, 1, 0))
            misses.append(values[span] - low_dot(keys[span], start, 1, 1))
        miss_grad = low_dot(inverse, jnp.concatenate(update_grads, axis=0), 0, 0)
        miss = jnp.concatenate(misses, axis=0)
        system_grad = jnp.where(strict, -low_dot(miss_grad, update, 1, 1), 0.0)
        strength_grads[index] = jnp.sum(miss_grad * miss, -1, keepdims=True) + jnp.sum(
            system_grad * gram, -1, keepdims=True
        )
        gram_grad = (strength * system_grad).astype(BF16)
        value_grad = strength * miss_grad
        value_low = value_grad.astype(BF16)
        value_grads[index] = value_grad
        query_grads[index] = jnp.concatenate(query_carried, axis=0) + low_dot(score_grad, keys, 1, 0)
        key_grad = jnp.concatenate(key_carried, axis=0) + low_dot(score_grad, queries, 0, 0)
        key_grad = key_grad + low_dot(gram_grad, keys, 1, 0) + low_dot(gram_grad, keys, 0, 0)
        key_state = [
            low_dot(value_low[head * BLOCK : (head + 1) * BLOCK], starts[head], 1, 0)
            for head in range(heads)
        ]
        key_grads[index] = key_grad - jnp.concatenate(key_state, axis=0)
    grads = [query_grads, key_grads, value_grads]
    logit_grads = []
    for head in range(heads):
        span = slice(head * BLOCK, (head + 1) * BLOCK)
        gate = gates[head]
        pulled = jnp.concatenate([strength_grads[index][span] for index in range(blocks)], axis=0)
        logit_grads.append(pulled * valid * gate * (1.0 - gate))
        for part in range(3):
            pulled = jnp.concatenate([grads[part][index][span] for index in range(blocks)], axis=0)
            total, shifted, taps = conv_part(
                proj_ref, before_ref, conv_ref, reach, part, head, head_dim, heads
            )
            gate_part = sigmoid(total)
            value = total * gate_part
            if part < 2:
                scale = lax.rsqrt(jnp.sum(value * value, -1, keepdims=True) + NORM_EPS)
                normed = value * scale
                pulled = scale * (pulled - normed * jnp.sum(normed * pulled, -1, keepdims=True))
                if part == 0:
                    pulled = pulled * head_dim ** (-0.5)
            pre_grad = pulled * gate_part * (1.0 + total * (1.0 - gate_part))
            column = slice(part * width + head * head_dim, part * width + (head + 1) * head_dim)
            tap_column = slice(head * head_dim, (head + 1) * head_dim)
            for lag in range(4):
                conv_grad_ref[part * 4 + lag : part * 4 + lag + 1, tap_column] += jnp.sum(
                    pre_grad * shifted[lag], 0, keepdims=True
                )
            joined = jnp.concatenate([pre_grad, halo_ref[:, column]], axis=0)
            total_grad = taps[0] * pre_grad
            for lag in range(1, 4):
                total_grad = total_grad + taps[lag] * (joined * reach_ahead[lag])[lag : lag + rows]
            proj_grad_ref[:, column] = total_grad.astype(BF16)
            halo_ref[:, column] = pre_grad[:HALO]
    blank = jnp.zeros((rows, LANES - heads), F32)
    proj_grad_ref[:, 3 * width :] = jnp.concatenate(logit_grads + [blank], axis=1).astype(BF16)


def mixer_specs(rows, columns, order):
    blocks = rows // BLOCK
    ratio = rows // HALO

    def whole(*shape):
        return pl.BlockSpec(shape, lambda step: (0,) * len(shape))

    def by_rows(size, column=0):
        return pl.BlockSpec((rows, size), lambda step: (order(step), column))

    def by_blocks(*tail):
        return pl.BlockSpec((blocks,) + tail, lambda step: (order(step),) + (0,) * len(tail))

    before = pl.BlockSpec(
        (HALO, columns), lambda step: (jnp.maximum(order(step) * ratio - 1, 0), 0)
    )
    return whole, by_rows, by_blocks, before


def mixer_forward(projected, conv_rows, head_gain, pos, valid, heads):
    slots = projected.shape[0]
    head_dim = head_gain.shape[1]
    width = heads * head_dim
    columns = 3 * width
    rows = slots // lax.axis_size("tensor")
    steps = slots // rows
    stacked = heads * BLOCK
    block_count = slots // BLOCK
    whole, by_rows, by_blocks, before = mixer_specs(rows, columns, lambda step: step)
    return pl.pallas_call(
        lambda *refs: forward_kernel(*refs, heads=heads, head_dim=head_dim),
        grid=(steps,),
        in_specs=[
            by_rows(columns),
            before,
            by_rows(LANES, columns // LANES),
            by_rows(1),
            by_rows(1),
            whole(12, width),
            whole(1, head_dim),
        ],
        out_specs=[
            by_rows(width),
            by_rows(width),
            by_blocks(heads, head_dim, head_dim),
            by_blocks(stacked, stacked),
            by_blocks(stacked, head_dim),
            by_blocks(stacked, head_dim),
        ],
        scratch_shapes=[pltpu.VMEM((heads, head_dim, head_dim), F32)],
        out_shape=[
            jax.ShapeDtypeStruct((slots, width), BF16),
            jax.ShapeDtypeStruct((slots, width), F32),
            jax.ShapeDtypeStruct((block_count, heads, head_dim, head_dim), BF16),
            jax.ShapeDtypeStruct((block_count, stacked, stacked), BF16),
            jax.ShapeDtypeStruct((block_count, stacked, head_dim), BF16),
            jax.ShapeDtypeStruct((block_count, stacked, head_dim), BF16),
        ],
        name="mixer_forward",
    )(projected, projected, projected, pos, valid, conv_rows, head_gain)


def mixer_backward(projected, conv_rows, head_gain, pos, valid, heads, kept, mixed_grad):
    slots = projected.shape[0]
    head_dim = head_gain.shape[1]
    width = heads * head_dim
    columns = 3 * width
    rows = slots // lax.axis_size("tensor")
    steps = slots // rows
    stacked = heads * BLOCK
    ratio = rows // HALO
    recall, start, inverse, update, weighted = kept
    pos_padded = jnp.pad(pos, ((0, HALO), (0, 0)))
    whole, by_rows, by_blocks, before = mixer_specs(rows, columns, lambda step: steps - 1 - step)
    return pl.pallas_call(
        lambda *refs: backward_kernel(*refs, heads=heads, head_dim=head_dim),
        grid=(steps,),
        in_specs=[
            by_rows(columns),
            before,
            by_rows(LANES, columns // LANES),
            by_rows(1),
            pl.BlockSpec((HALO, 1), lambda step: ((steps - step) * ratio, 0)),
            by_rows(1),
            whole(12, width),
            whole(1, head_dim),
            by_rows(width),
            by_blocks(heads, head_dim, head_dim),
            by_blocks(stacked, stacked),
            by_blocks(stacked, head_dim),
            by_blocks(stacked, head_dim),
            by_rows(width),
        ],
        out_specs=[by_rows(columns + LANES), whole(12, width), whole(1, head_dim)],
        scratch_shapes=[
            pltpu.VMEM((heads, head_dim, head_dim), F32),
            pltpu.VMEM((HALO, columns), F32),
        ],
        out_shape=[
            jax.ShapeDtypeStruct((slots, columns + LANES), BF16),
            jax.ShapeDtypeStruct((12, width), F32),
            jax.ShapeDtypeStruct((1, head_dim), F32),
        ],
        name="mixer_backward",
    )(
        projected, projected, projected, pos, pos_padded, valid, conv_rows, head_gain,
        recall, start, inverse, update, weighted, mixed_grad,
    )


def doc_layout(length_pair, slot_count):
    first_end = (length_pair[0] + BLOCK - 1) // BLOCK * BLOCK
    second_end = first_end + (length_pair[1] + BLOCK - 1) // BLOCK * BLOCK
    places = jnp.arange(slot_count, dtype=jnp.int32)
    in_first = places < first_end
    in_second = jnp.logical_and(places >= first_end, places < second_end)
    doc_begin = jnp.where(in_first, 0, jnp.where(in_second, first_end, second_end))
    doc_limit = jnp.where(in_first, length_pair[0], jnp.where(in_second, length_pair[1], 0))
    offset = places - doc_begin
    is_valid = (offset < doc_limit).astype(F32)
    return offset.astype(F32)[:, None], is_valid[:, None]


def ring_shift(value, step):
    size = lax.axis_size("tensor")
    return lax.ppermute(value, "tensor", [(place, (place + step) % size) for place in range(size)])


def held(value, *others):
    return lax.optimization_barrier((value, others))[0]


def piece_start(step, count):
    size = lax.axis_size("tensor")
    return lax.rem(lax.axis_index("tensor") + step, size) * count


def gather_rows(rows, *token, mid=()):
    size = lax.axis_size("tensor")
    count = rows.shape[0]
    half = count // 2
    rows = held(rows, token)
    full = jnp.zeros((size * count, rows.shape[1]), rows.dtype)

    def put(full, piece, step, at=0):
        return lax.dynamic_update_slice(full, piece, (piece_start(step, count) + at, 0))

    full = put(full, rows, 0)
    from_left = rows
    from_right = rows
    for step in range(1, size // 2):
        from_left = ring_shift(from_left, 1)
        from_right = ring_shift(from_right, -1)
        full = put(full, from_left, size - step)
        full = put(full, from_right, step)
    from_left_half, from_right_half = from_left[:half], from_right[half:]
    if mid:
        from_left_half, from_right_half = held((from_left_half, from_right_half), mid)
    far = ring_shift(from_left_half, 1), ring_shift(from_right_half, -1)
    full = put(full, far[0], size // 2)
    full = put(full, far[1], size // 2, half)
    return full, (from_left, from_right), far


def scatter_rows(partial, *token, mid=()):
    size = lax.axis_size("tensor")
    count = partial.shape[0] // size
    half = count // 2
    low = held(partial, token)

    def take(step, at=0, length=count):
        start = piece_start(step, count) + at
        return lax.dynamic_slice(low, (start, 0), (length, low.shape[1])).astype(F32)

    to_right = ring_shift(take(size // 2, 0, half).astype(BF16), 1)
    to_left = ring_shift(take(size // 2, half, half).astype(BF16), -1)
    first = to_right, to_left
    if mid:
        to_right, to_left = held(first, mid)
    for step in range(size // 2 - 1, 0, -1):
        right = take(step)
        left = take(size - step)
        if step == size // 2 - 1:
            right = joined([right[:half] + to_right.astype(F32), right[half:]])
            left = joined([left[:half], left[half:] + to_left.astype(F32)])
        else:
            right = right + to_right.astype(F32)
            left = left + to_left.astype(F32)
        to_right = ring_shift(right.astype(BF16), 1)
        to_left = ring_shift(left.astype(BF16), -1)
    total = take(0) + to_right.astype(F32) + to_left.astype(F32)
    return total, first, (to_right, to_left)


def dot(left, right, left_dim, right_dim, out_type=F32):
    return lax.dot_general(
        left, right, (((left_dim,), (right_dim,)), ((), ())), preferred_element_type=out_type
    )


def gather_dp(value):
    return lax.all_gather(value, "dp", axis=0, tiled=True)


def scatter_dp(value):
    return lax.psum_scatter(value, "dp", scatter_dimension=0, tiled=True)


def row_scale(values):
    return lax.rsqrt(jnp.mean(values * values, -1, keepdims=True) + NORM_EPS)


def norm_pull(values, pulled):
    scale = row_scale(values)
    normed = values * scale
    return scale * (pulled - normed * jnp.mean(normed * pulled, -1, keepdims=True))


def joined(parts):
    return jnp.concatenate(parts, axis=0)


def per_device(
    tokens, cotangent, doc_lengths, attn_gain, w_qkv, w_beta, conv_weight, head_gain,
    w_out, ffn_gain, w_gate_up, w_down,
):
    batches, local_rows, width = tokens.shape
    size = lax.axis_size("tensor")
    dp_size = lax.axis_size("dp")
    slots = local_rows * size
    shard = w_qkv.shape[0]
    heads = w_beta.shape[1]
    units = w_down.shape[0]
    head_share = head_gain.shape[0]
    head_dim = head_share * dp_size
    columns = 3 * heads * head_dim
    conv_share = 12 * heads * head_share
    small_share = conv_share + head_share
    extra = -(-small_share // shard)
    small_at = columns + heads

    attn_column = attn_gain.astype(F32)[:, None]
    ffn_column = ffn_gain.astype(F32)[:, None]
    qkv_rows = jnp.concatenate([w_qkv.reshape(shard, columns), w_beta], axis=1).astype(F32)
    small = jnp.concatenate(
        [conv_weight.reshape(-1), head_gain, jnp.zeros((extra * shard - small_share,), BF16)]
    ).reshape(shard, extra)
    blank = jnp.zeros((shard, LANES - heads - extra), BF16)
    full_proj = gather_dp(
        jnp.concatenate([(attn_column * qkv_rows).astype(BF16), small, blank], axis=1)
    )
    full_out = gather_dp(w_out.T)
    gate_up_rows = w_gate_up.reshape(shard, 2 * units).astype(F32)
    full_gate_up = gather_dp((ffn_column * gate_up_rows).astype(BF16))
    full_down = gather_dp(w_down.T)
    small = full_proj[:, small_at : small_at + extra].astype(F32).reshape(dp_size, extra * shard)
    full_conv = small[:, :conv_share].reshape(dp_size, 12, heads, head_share)
    full_conv = jnp.transpose(full_conv, (1, 2, 0, 3)).reshape(12, heads * head_dim)
    full_head_gain = small[:, conv_share:small_share].reshape(1, head_dim)

    rows = [tokens[index].astype(F32) for index in range(batches)]
    layouts = [doc_layout(doc_lengths[index, 0], slots) for index in range(batches)]

    def mix(index, projected):
        mixed, *kept = mixer_forward(
            projected, full_conv, full_head_gain, *layouts[index], heads
        )
        return mixed, kept, dot(mixed, full_out, 1, 1, BF16)

    def after_mixer(index, branch):
        hidden = rows[index] + branch
        return hidden, (hidden * row_scale(hidden)).astype(BF16)

    def feed(ffn_full):
        gate_up = dot(ffn_full, full_gate_up, 1, 0)
        gate = gate_up[:, :units]
        activated = (gate * sigmoid(gate) * gate_up[:, units:]).astype(BF16)
        return gate_up, activated

    def feed_back(gate_up, cot_full):
        grad_act = dot(cot_full, full_down, 1, 0)
        gate = gate_up[:, :units]
        up = gate_up[:, units:]
        opened = sigmoid(gate)
        grad_gate = grad_act * up * opened * (1.0 + gate * (1.0 - opened))
        grad_up = grad_act * (gate * opened)
        grad_gate_up = jnp.concatenate([grad_gate, grad_up], axis=1).astype(BF16)
        return grad_gate_up, dot(grad_gate_up, full_gate_up, 1, 1, BF16)

    def before_ffn(index, hidden, pulled):
        return cotangent[index].astype(F32) + norm_pull(hidden, pulled)

    def mix_back(index, grad_mixed, projected, kept):
        grad_proj, conv_grad, gain_grad = mixer_backward(
            projected, full_conv, full_head_gain, *layouts[index], heads, kept, grad_mixed
        )
        return grad_proj, conv_grad, gain_grad, dot(grad_proj, full_proj, 1, 1, BF16)

    attn_in = [(rows[index] * row_scale(rows[index])).astype(BF16) for index in range(batches)]
    attn_0, first, last = gather_rows(attn_in[0])
    attn_1, first, last = gather_rows(attn_in[1], last)
    proj_0 = dot(held(attn_0, first), full_proj, 1, 0)
    cot_0, cot_first, last = gather_rows(cotangent[0], first, proj_0)
    mixed_0, kept_0, part_0 = mix(0, held(proj_0, attn_1))

    proj_1 = dot(held(attn_1, part_0), full_proj, 1, 0)
    branch, first, last = scatter_rows(part_0, mid=(proj_1,))
    cot_1, cot_first, cot_last = gather_rows(cotangent[1], first, cot_first)
    mixed_1, kept_1, part_1 = mix(1, held(proj_1, first, cot_0))
    hidden_0, ffn_in = after_mixer(0, branch)

    ffn_0, first, last = gather_rows(ffn_in, cot_first, part_1, full_gate_up)
    gate_up_0, act_0 = feed(ffn_0)
    branch, first, last = scatter_rows(part_1, first, mid=(gate_up_0, full_down))
    grad_gate_up_0, part_0 = feed_back(gate_up_0, cot_0)
    hidden_1, ffn_in = after_mixer(1, branch)

    ffn_1, ffn_first, last = gather_rows(ffn_in, part_0)
    pulled, first, last = scatter_rows(part_0, ffn_first)
    down_0 = dot(held(act_0, ffn_first), full_down, 1, 1, BF16)
    down_grad = dot(held(cot_0, down_0), act_0, 0, 0, BF16)
    gate_up_grad = dot(held(ffn_0, down_grad), grad_gate_up_0, 0, 0, BF16)
    gate_up_1, act_1 = feed(held(ffn_1, first, gate_up_grad))
    grad_gate_up_1, part_1 = feed_back(gate_up_1, cot_1)
    grad_hidden_0 = before_ffn(0, hidden_0, pulled)

    branch_0, first, last = gather_rows(grad_hidden_0.astype(BF16))
    act_1_held = held(act_1, part_1, first)
    down_1 = dot(act_1_held, full_down, 1, 1, BF16)
    down_grad = (down_grad + dot(cot_1, act_1_held, 0, 0)).astype(BF16)
    gate_up_grad = gate_up_grad + dot(held(ffn_1, down_1, down_grad), grad_gate_up_1, 0, 0)
    gate_up_grad = gate_up_grad.astype(BF16)
    pulled, first, last = scatter_rows(part_1, first, mid=(gate_up_grad,))
    grad_hidden_1 = before_ffn(1, hidden_1, pulled)
    down_grad = scatter_dp(down_grad)

    branch_in = held(grad_hidden_1.astype(BF16), gate_up_grad)
    branch_1, first, last = gather_rows(branch_in)
    gate_up_grad = scatter_dp(gate_up_grad)
    grad_mixed = dot(held(branch_0, branch_in), full_out, 1, 0)
    grad_proj_0, conv_grad_0, gain_grad_0, part_0 = mix_back(0, grad_mixed, proj_0, kept_0)
    lower_0, down_first, down_last = scatter_rows(down_0, branch_in, mid=(part_0,))

    pulled, first, last = scatter_rows(part_0, last)
    out_grad = dot(
        joined([held(branch_0, part_0), branch_1]), joined([mixed_0, mixed_1]), 0, 0, BF16
    )
    grad_mixed = dot(held(branch_1, part_0), full_out, 1, 0)
    input_rows_0 = grad_hidden_0 + norm_pull(rows[0], pulled)
    grad_mixed = held(grad_mixed, first, down_first, out_grad)
    grad_proj_1, conv_grad_1, gain_grad_1, part_1 = mix_back(1, grad_mixed, proj_1, kept_1)

    attn_all = joined([held(attn_0, part_1, last, down_last), attn_1])
    pulled, first, last = scatter_rows(part_1, last, down_last, down_grad)
    proj_grad = dot(attn_all, joined([grad_proj_0, grad_proj_1]), 0, 0, BF16)
    conv_grad = (conv_grad_0 + conv_grad_1).reshape(12, heads, dp_size, head_share)
    conv_grad = jnp.transpose(conv_grad, (2, 0, 1, 3)).reshape(dp_size, conv_share)
    head_gain_grad = (gain_grad_0 + gain_grad_1).reshape(dp_size, head_share)
    small_grad = jnp.concatenate(
        [conv_grad, head_gain_grad, jnp.zeros((dp_size, extra * shard - small_share), F32)], axis=1
    )
    small_grad = small_grad.reshape(dp_size * shard, extra).astype(BF16)
    small_grad = jnp.pad(small_grad, ((0, 0), (small_at, LANES - heads - extra)))
    mixer_grad = scatter_dp(jnp.concatenate([proj_grad + small_grad, out_grad], axis=1))
    lower_1, first, last = scatter_rows(down_1, last, gate_up_grad)
    mixer_grad = held(mixer_grad, last)
    input_rows_1 = grad_hidden_1 + norm_pull(rows[1], pulled)
    layer_rows_0 = (hidden_0 + lower_0).astype(BF16)
    layer_rows_1 = (hidden_1 + lower_1).astype(BF16)

    proj_grad = mixer_grad[:, : columns + LANES].astype(F32)
    out_grad = mixer_grad[:, columns + LANES :]
    gate_up_grad = gate_up_grad.astype(F32)
    small_grad = proj_grad[:, small_at : small_at + extra].reshape(extra * shard)
    gain_grads = jnp.concatenate(
        [
            jnp.sum(proj_grad[:, :small_at] * qkv_rows, axis=1),
            jnp.sum(gate_up_grad * gate_up_rows, axis=1),
            small_grad[conv_share:small_share],
        ]
    )[None]
    total = gain_grads
    for step in range(1, size):
        total = total + ring_shift(gain_grads, step)
    total = total[0]
    proj_grad = proj_grad[:, :small_at] * attn_column
    return (
        jnp.stack([layer_rows_0, layer_rows_1]),
        jnp.stack([input_rows_0, input_rows_1]),
        total[:shard],
        proj_grad[:, :columns].reshape(shard, 3, -1),
        proj_grad[:, columns:],
        small_grad[:conv_share].reshape(3, 4, heads, head_share),
        total[2 * shard :],
        out_grad.T.astype(F32),
        total[shard : 2 * shard],
        (gate_up_grad * ffn_column).reshape(shard, 2, units),
        down_grad.T.astype(F32),
    )


def solution(mesh):
    return jax.shard_map(
        per_device,
        mesh=mesh,
        in_specs=(
            P(None, ("dp", "tensor"), None),
            P(None, ("dp", "tensor"), None),
            P(None, "dp", None),
            P("dp"),
            P("dp", None, "tensor"),
            P("dp", "tensor"),
            P(None, None, "tensor", "dp"),
            P("dp"),
            P("tensor", "dp"),
            P("dp"),
            P("dp", None, "tensor"),
            P("tensor", "dp"),
        ),
        out_specs=(
            P(None, ("dp", "tensor"), None),
            P(None, ("dp", "tensor"), None),
            P("dp"),
            P("dp", None, "tensor"),
            P("dp", "tensor"),
            P(None, None, "tensor", "dp"),
            P("dp"),
            P("tensor", "dp"),
            P("dp"),
            P("dp", None, "tensor"),
            P("tensor", "dp"),
        ),
        check_vma=False,
    )
```

```python
import jax
import jax.numpy as jnp
from jax import lax
from jax.experimental import pallas as pl
from jax.experimental.pallas import tpu as pltpu
from jax.sharding import PartitionSpec as P

BLOCK = 64
NORM_EPS = 1e-06
HEAD_EPS = 1e-05
F32 = jnp.float32
BF16 = jnp.bfloat16
LANES = 128
HALO = 8


def low_dot(left, right, left_dim, right_dim):
    return lax.dot_general(
        left.astype(BF16),
        right.astype(BF16),
        (((left_dim,), (right_dim,)), ((), ())),
        preferred_element_type=F32,
    )


def sigmoid(value):
    return 1.0 / (1.0 + jnp.exp(-value))


def block_masks(rows):
    row = lax.broadcasted_iota(jnp.int32, (rows, rows), 0)
    col = lax.broadcasted_iota(jnp.int32, (rows, rows), 1)
    same = {size: (row // size) == (col // size) for size in (8, 16, 32, 64)}
    strict = jnp.logical_and(same[64], col < row)
    lower = jnp.logical_and(same[64], col <= row)
    eye = (row == col).astype(F32)
    return same, strict, lower, eye


def unit_inverse(system, same, eye):
    base = jnp.where(same[8], system, 0.0)
    square = low_dot(base, base, 1, 0)
    fourth = low_dot(square, square, 1, 0)
    inverse = eye - base
    inverse = inverse + low_dot(inverse, square, 1, 0)
    inverse = inverse + low_dot(inverse, fourth, 1, 0)
    for size in (8, 16, 32):
        off = jnp.where(jnp.logical_and(same[2 * size], jnp.logical_not(same[size])), system, 0.0)
        inverse = inverse - low_dot(inverse, low_dot(off, inverse, 1, 0), 1, 0)
    return inverse


def delayed_rows(previous, current, lag):
    if lag == 0:
        return current
    rows = current.shape[0]
    joined = jnp.concatenate([previous, current], axis=0)
    return joined[HALO - lag : HALO - lag + rows]


def conv_part(proj_ref, before_ref, conv_ref, reach, part, head, head_dim, heads):
    width = heads * head_dim
    column = part * width + head * head_dim
    current = proj_ref[:, column : column + head_dim]
    previous = before_ref[:, column : column + head_dim]
    taps = [conv_ref[part * 4 + lag : part * 4 + lag + 1, head * head_dim : (head + 1) * head_dim] for lag in range(4)]
    shifted = [current]
    for lag in range(1, 4):
        shifted.append(delayed_rows(previous, current, lag) * reach[lag])
    total = taps[0] * shifted[0]
    for lag in range(1, 4):
        total = total + taps[lag] * shifted[lag]
    return total, shifted, taps


def stack_heads(pieces, index):
    return jnp.concatenate([piece[index * BLOCK : (index + 1) * BLOCK] for piece in pieces], axis=0)


def forward_kernel(
    proj_ref, before_ref, logit_ref, pos_ref, valid_ref, conv_ref, gain_ref,
    mixed_ref, recall_ref, start_ref, inverse_ref, update_ref, weight_ref,
    state_ref, *, heads, head_dim,
):
    rows = proj_ref.shape[0]
    blocks = rows // BLOCK
    stacked = heads * BLOCK

    @pl.when(pl.program_id(0) == 0)
    def _():
        state_ref[...] = jnp.zeros_like(state_ref)

    pos = pos_ref[...]
    valid = valid_ref[...]
    reach = [None] + [(pos >= lag).astype(F32) for lag in range(1, 4)]
    parts = [[], [], []]
    strengths = []
    for head in range(heads):
        for part in range(3):
            total, _, _ = conv_part(proj_ref, before_ref, conv_ref, reach, part, head, head_dim, heads)
            value = total * sigmoid(total)
            if part < 2:
                scale = lax.rsqrt(jnp.sum(value * value, -1, keepdims=True) + NORM_EPS)
                if part == 0:
                    scale = scale * head_dim ** (-0.5)
                value = value * scale
            parts[part].append(value)
        strengths.append(sigmoid(logit_ref[:, head : head + 1]) * valid)
    same, strict, lower, eye = block_masks(stacked)
    local = []
    for index in range(blocks):
        queries = stack_heads(parts[0], index).astype(BF16)
        keys = stack_heads(parts[1], index)
        values = stack_heads(parts[2], index)
        strength = stack_heads(strengths, index)
        keys_low = keys.astype(BF16)
        gram = low_dot(keys_low, keys_low, 1, 1)
        system = jnp.where(strict, strength * gram, 0.0)
        inverse = unit_inverse(system, same, eye).astype(BF16)
        weighted = low_dot(inverse, strength * keys, 1, 0).astype(BF16)
        fresh = low_dot(inverse, strength * values, 1, 0)
        scores = jnp.where(lower, low_dot(queries, keys_low, 1, 1), 0.0).astype(BF16)
        inverse_ref[index] = inverse
        weight_ref[index] = weighted
        local.append((queries, keys_low, weighted, fresh, scores))
    for index in range(blocks):
        queries, keys_low, weighted, fresh, scores = local[index]
        keep = (pos[index * BLOCK : index * BLOCK + 1] != 0).astype(F32)
        updates = []
        carried = []
        for head in range(heads):
            span = slice(head * BLOCK, (head + 1) * BLOCK)
            state = state_ref[head] * keep
            state_low = state.astype(BF16)
            start_ref[index, head] = state_low
            update = fresh[span] - low_dot(weighted[span], state_low, 1, 1)
            update_low = update.astype(BF16)
            updates.append(update_low)
            carried.append(low_dot(queries[span], state_low, 1, 1))
            state_ref[head] = state + low_dot(update_low, keys_low[span], 0, 0)
        update_all = jnp.concatenate(updates, axis=0)
        update_ref[index] = update_all
        recall_all = jnp.concatenate(carried, axis=0) + low_dot(scores, update_all, 1, 0)
        scale = lax.rsqrt(jnp.mean(recall_all * recall_all, -1, keepdims=True) + HEAD_EPS)
        normed = recall_all * scale * gain_ref[...]
        here = slice(index * BLOCK, (index + 1) * BLOCK)
        for head in range(heads):
            span = slice(head * BLOCK, (head + 1) * BLOCK)
            column = slice(head * head_dim, (head + 1) * head_dim)
            recall_ref[here, column] = recall_all[span]
            mixed_ref[here, column] = (normed[span] * valid[here]).astype(BF16)


def backward_kernel(
    proj_ref, before_ref, logit_ref, pos_ref, after_ref, valid_ref, conv_ref, gain_ref,
    recall_ref, start_ref, inverse_ref, update_ref, weight_ref, mixed_grad_ref,
    proj_grad_ref, conv_grad_ref, gain_grad_ref,
    state_ref, halo_ref, *, heads, head_dim,
):
    rows = proj_ref.shape[0]
    blocks = rows // BLOCK
    stacked = heads * BLOCK
    width = heads * head_dim

    @pl.when(pl.program_id(0) == 0)
    def _():
        state_ref[...] = jnp.zeros_like(state_ref)
        halo_ref[...] = jnp.zeros_like(halo_ref)
        conv_grad_ref[...] = jnp.zeros_like(conv_grad_ref)
        gain_grad_ref[...] = jnp.zeros_like(gain_grad_ref)

    pos = pos_ref[...]
    valid = valid_ref[...]
    reach = [None] + [(pos >= lag).astype(F32) for lag in range(1, 4)]
    pos_ahead = jnp.concatenate([pos, after_ref[...]], axis=0)
    reach_ahead = [None] + [(pos_ahead >= lag).astype(F32) for lag in range(1, 4)]
    gain = gain_ref[...]
    parts = [[], [], []]
    gates = []
    recall_grads = []
    gain_grad = jnp.zeros((1, head_dim), F32)
    for head in range(heads):
        for part in range(3):
            total, _, _ = conv_part(proj_ref, before_ref, conv_ref, reach, part, head, head_dim, heads)
            value = total * sigmoid(total)
            if part < 2:
                scale = lax.rsqrt(jnp.sum(value * value, -1, keepdims=True) + NORM_EPS)
                if part == 0:
                    scale = scale * head_dim ** (-0.5)
                value = value * scale
            parts[part].append(value)
        gates.append(sigmoid(logit_ref[:, head : head + 1]))
        column = slice(head * head_dim, (head + 1) * head_dim)
        recall = recall_ref[:, column]
        pulled = mixed_grad_ref[:, column] * valid
        scale = lax.rsqrt(jnp.mean(recall * recall, -1, keepdims=True) + HEAD_EPS)
        normed = recall * scale
        gain_grad = gain_grad + jnp.sum(pulled * normed, 0, keepdims=True)
        pulled = pulled * gain
        recall_grads.append(
            scale * (pulled - normed * jnp.mean(normed * pulled, -1, keepdims=True))
        )
    gain_grad_ref[...] += gain_grad
    strengths = [gate * valid for gate in gates]
    same, strict, lower, eye = block_masks(stacked)
    query_grads = [None] * blocks
    key_grads = [None] * blocks
    value_grads = [None] * blocks
    strength_grads = [None] * blocks
    for index in range(blocks - 1, -1, -1):
        queries = stack_heads(parts[0], index).astype(BF16)
        keys = stack_heads(parts[1], index).astype(BF16)
        values = stack_heads(parts[2], index)
        strength = stack_heads(strengths, index)
        out_grad = stack_heads(recall_grads, index).astype(BF16)
        inverse = inverse_ref[index]
        weighted = weight_ref[index]
        update = update_ref[index]
        gram = low_dot(keys, keys, 1, 1)
        scores = jnp.where(lower, low_dot(queries, keys, 1, 1), 0.0).astype(BF16)
        local_grad = low_dot(scores, out_grad, 0, 0)
        score_grad = jnp.where(lower, low_dot(out_grad, update, 1, 1), 0.0).astype(BF16)
        keep = (pos[index * BLOCK : index * BLOCK + 1] != 0).astype(F32)
        update_grads = []
        query_carried = []
        key_carried = []
        misses = []
        starts = []
        for head in range(heads):
            span = slice(head * BLOCK, (head + 1) * BLOCK)
            ahead = state_ref[head]
            ahead_low = ahead.astype(BF16)
            start = start_ref[index, head]
            starts.append(start)
            update_grad = local_grad[span] + low_dot(keys[span], ahead_low, 1, 1)
            update_grad_low = update_grad.astype(BF16)
            update_grads.append(update_grad_low)
            carried = ahead + low_dot(out_grad[span], queries[span], 0, 0)
            carried = carried - low_dot(update_grad_low, weighted[span], 0, 0)
            state_ref[head] = carried * keep
            query_carried.append(low_dot(out_grad[span], start, 1, 0))
            key_carried.append(low_dot(update[span], ahead_low, 1, 0))
            misses.append(values[span] - low_dot(keys[span], start, 1, 1))
        miss_grad = low_dot(inverse, jnp.concatenate(update_grads, axis=0), 0, 0)
        miss = jnp.concatenate(misses, axis=0)
        system_grad = jnp.where(strict, -low_dot(miss_grad, update, 1, 1), 0.0)
        strength_grads[index] = jnp.sum(miss_grad * miss, -1, keepdims=True) + jnp.sum(
            system_grad * gram, -1, keepdims=True
        )
        gram_grad = (strength * system_grad).astype(BF16)
        value_grad = strength * miss_grad
        value_low = value_grad.astype(BF16)
        value_grads[index] = value_grad
        query_grads[index] = jnp.concatenate(query_carried, axis=0) + low_dot(score_grad, keys, 1, 0)
        key_grad = jnp.concatenate(key_carried, axis=0) + low_dot(score_grad, queries, 0, 0)
        key_grad = key_grad + low_dot(gram_grad, keys, 1, 0) + low_dot(gram_grad, keys, 0, 0)
        key_state = [
            low_dot(value_low[head * BLOCK : (head + 1) * BLOCK], starts[head], 1, 0)
            for head in range(heads)
        ]
        key_grads[index] = key_grad - jnp.concatenate(key_state, axis=0)
    grads = [query_grads, key_grads, value_grads]
    logit_grads = []
    for head in range(heads):
        span = slice(head * BLOCK, (head + 1) * BLOCK)
        gate = gates[head]
        pulled = jnp.concatenate([strength_grads[index][span] for index in range(blocks)], axis=0)
        logit_grads.append(pulled * valid * gate * (1.0 - gate))
        for part in range(3):
            pulled = jnp.concatenate([grads[part][index][span] for index in range(blocks)], axis=0)
            total, shifted, taps = conv_part(
                proj_ref, before_ref, conv_ref, reach, part, head, head_dim, heads
            )
            gate_part = sigmoid(total)
            value = total * gate_part
            if part < 2:
                scale = lax.rsqrt(jnp.sum(value * value, -1, keepdims=True) + NORM_EPS)
                normed = value * scale
                pulled = scale * (pulled - normed * jnp.sum(normed * pulled, -1, keepdims=True))
                if part == 0:
                    pulled = pulled * head_dim ** (-0.5)
            pre_grad = pulled * gate_part * (1.0 + total * (1.0 - gate_part))
            column = slice(part * width + head * head_dim, part * width + (head + 1) * head_dim)
            tap_column = slice(head * head_dim, (head + 1) * head_dim)
            for lag in range(4):
                conv_grad_ref[part * 4 + lag : part * 4 + lag + 1, tap_column] += jnp.sum(
                    pre_grad * shifted[lag], 0, keepdims=True
                )
            joined = jnp.concatenate([pre_grad, halo_ref[:, column]], axis=0)
            total_grad = taps[0] * pre_grad
            for lag in range(1, 4):
                total_grad = total_grad + taps[lag] * (joined * reach_ahead[lag])[lag : lag + rows]
            proj_grad_ref[:, column] = total_grad.astype(BF16)
            halo_ref[:, column] = pre_grad[:HALO]
    blank = jnp.zeros((rows, LANES - heads), F32)
    proj_grad_ref[:, 3 * width :] = jnp.concatenate(logit_grads + [blank], axis=1).astype(BF16)


def mixer_specs(rows, columns, order):
    blocks = rows // BLOCK
    ratio = rows // HALO

    def whole(*shape):
        return pl.BlockSpec(shape, lambda step: (0,) * len(shape))

    def by_rows(size, column=0):
        return pl.BlockSpec((rows, size), lambda step: (order(step), column))

    def by_blocks(*tail):
        return pl.BlockSpec((blocks,) + tail, lambda step: (order(step),) + (0,) * len(tail))

    before = pl.BlockSpec(
        (HALO, columns), lambda step: (jnp.maximum(order(step) * ratio - 1, 0), 0)
    )
    return whole, by_rows, by_blocks, before


def mixer_forward(projected, conv_rows, head_gain, pos, valid, heads):
    slots = projected.shape[0]
    head_dim = head_gain.shape[1]
    width = heads * head_dim
    columns = 3 * width
    rows = slots // lax.axis_size("tensor")
    steps = slots // rows
    stacked = heads * BLOCK
    block_count = slots // BLOCK
    whole, by_rows, by_blocks, before = mixer_specs(rows, columns, lambda step: step)
    return pl.pallas_call(
        lambda *refs: forward_kernel(*refs, heads=heads, head_dim=head_dim),
        grid=(steps,),
        in_specs=[
            by_rows(columns),
            before,
            by_rows(LANES, columns // LANES),
            by_rows(1),
            by_rows(1),
            whole(12, width),
            whole(1, head_dim),
        ],
        out_specs=[
            by_rows(width),
            by_rows(width),
            by_blocks(heads, head_dim, head_dim),
            by_blocks(stacked, stacked),
            by_blocks(stacked, head_dim),
            by_blocks(stacked, head_dim),
        ],
        scratch_shapes=[pltpu.VMEM((heads, head_dim, head_dim), F32)],
        out_shape=[
            jax.ShapeDtypeStruct((slots, width), BF16),
            jax.ShapeDtypeStruct((slots, width), F32),
            jax.ShapeDtypeStruct((block_count, heads, head_dim, head_dim), BF16),
            jax.ShapeDtypeStruct((block_count, stacked, stacked), BF16),
            jax.ShapeDtypeStruct((block_count, stacked, head_dim), BF16),
            jax.ShapeDtypeStruct((block_count, stacked, head_dim), BF16),
        ],
        name="mixer_forward",
    )(projected, projected, projected, pos, valid, conv_rows, head_gain)


def mixer_backward(projected, conv_rows, head_gain, pos, valid, heads, kept, mixed_grad):
    slots = projected.shape[0]
    head_dim = head_gain.shape[1]
    width = heads * head_dim
    columns = 3 * width
    rows = slots // lax.axis_size("tensor")
    steps = slots // rows
    stacked = heads * BLOCK
    ratio = rows // HALO
    recall, start, inverse, update, weighted = kept
    pos_padded = jnp.pad(pos, ((0, HALO), (0, 0)))
    whole, by_rows, by_blocks, before = mixer_specs(rows, columns, lambda step: steps - 1 - step)
    return pl.pallas_call(
        lambda *refs: backward_kernel(*refs, heads=heads, head_dim=head_dim),
        grid=(steps,),
        in_specs=[
            by_rows(columns),
            before,
            by_rows(LANES, columns // LANES),
            by_rows(1),
            pl.BlockSpec((HALO, 1), lambda step: ((steps - step) * ratio, 0)),
            by_rows(1),
            whole(12, width),
            whole(1, head_dim),
            by_rows(width),
            by_blocks(heads, head_dim, head_dim),
            by_blocks(stacked, stacked),
            by_blocks(stacked, head_dim),
            by_blocks(stacked, head_dim),
            by_rows(width),
        ],
        out_specs=[by_rows(columns + LANES), whole(12, width), whole(1, head_dim)],
        scratch_shapes=[
            pltpu.VMEM((heads, head_dim, head_dim), F32),
            pltpu.VMEM((HALO, columns), F32),
        ],
        out_shape=[
            jax.ShapeDtypeStruct((slots, columns + LANES), BF16),
            jax.ShapeDtypeStruct((12, width), F32),
            jax.ShapeDtypeStruct((1, head_dim), F32),
        ],
        name="mixer_backward",
    )(
        projected, projected, projected, pos, pos_padded, valid, conv_rows, head_gain,
        recall, start, inverse, update, weighted, mixed_grad,
    )


def doc_layout(length_pair, slot_count):
    first_end = (length_pair[0] + BLOCK - 1) // BLOCK * BLOCK
    second_end = first_end + (length_pair[1] + BLOCK - 1) // BLOCK * BLOCK
    places = jnp.arange(slot_count, dtype=jnp.int32)
    in_first = places < first_end
    in_second = jnp.logical_and(places >= first_end, places < second_end)
    doc_begin = jnp.where(in_first, 0, jnp.where(in_second, first_end, second_end))
    doc_limit = jnp.where(in_first, length_pair[0], jnp.where(in_second, length_pair[1], 0))
    offset = places - doc_begin
    is_valid = (offset < doc_limit).astype(F32)
    return offset.astype(F32)[:, None], is_valid[:, None]


def ring_shift(value, step):
    size = lax.axis_size("tensor")
    return lax.ppermute(value, "tensor", [(place, (place + step) % size) for place in range(size)])


def held(value, *others):
    return lax.optimization_barrier((value, others))[0]


def piece_start(step, count):
    size = lax.axis_size("tensor")
    return lax.rem(lax.axis_index("tensor") + step, size) * count


def gather_rows(rows, *token, mid=()):
    size = lax.axis_size("tensor")
    count = rows.shape[0]
    half = count // 2
    rows = held(rows, token)
    full = jnp.zeros((size * count, rows.shape[1]), rows.dtype)

    def put(full, piece, step, at=0):
        return lax.dynamic_update_slice(full, piece, (piece_start(step, count) + at, 0))

    full = put(full, rows, 0)
    from_left = rows
    from_right = rows
    for step in range(1, size // 2):
        from_left = ring_shift(from_left, 1)
        from_right = ring_shift(from_right, -1)
        full = put(full, from_left, size - step)
        full = put(full, from_right, step)
    from_left_half, from_right_half = from_left[:half], from_right[half:]
    if mid:
        from_left_half, from_right_half = held((from_left_half, from_right_half), mid)
    far = ring_shift(from_left_half, 1), ring_shift(from_right_half, -1)
    full = put(full, far[0], size // 2)
    full = put(full, far[1], size // 2, half)
    return full, (from_left, from_right), far


def scatter_rows(partial, *token, mid=()):
    size = lax.axis_size("tensor")
    count = partial.shape[0] // size
    half = count // 2
    low = held(partial, token)

    def take(step, at=0, length=count):
        start = piece_start(step, count) + at
        return lax.dynamic_slice(low, (start, 0), (length, low.shape[1])).astype(F32)

    to_right = ring_shift(take(size // 2, 0, half).astype(BF16), 1)
    to_left = ring_shift(take(size // 2, half, half).astype(BF16), -1)
    first = to_right, to_left
    if mid:
        to_right, to_left = held(first, mid)
    for step in range(size // 2 - 1, 0, -1):
        right = take(step)
        left = take(size - step)
        if step == size // 2 - 1:
            right = joined([right[:half] + to_right.astype(F32), right[half:]])
            left = joined([left[:half], left[half:] + to_left.astype(F32)])
        else:
            right = right + to_right.astype(F32)
            left = left + to_left.astype(F32)
        to_right = ring_shift(right.astype(BF16), 1)
        to_left = ring_shift(left.astype(BF16), -1)
    total = take(0) + to_right.astype(F32) + to_left.astype(F32)
    return total, first, (to_right, to_left)


def dot(left, right, left_dim, right_dim, out_type=F32):
    return lax.dot_general(
        left, right, (((left_dim,), (right_dim,)), ((), ())), preferred_element_type=out_type
    )


def gather_dp(value):
    return lax.all_gather(value, "dp", axis=0, tiled=True)


def scatter_dp(value):
    return lax.psum_scatter(value, "dp", scatter_dimension=0, tiled=True)


def row_scale(values):
    return lax.rsqrt(jnp.mean(values * values, -1, keepdims=True) + NORM_EPS)


def norm_pull(values, pulled):
    scale = row_scale(values)
    normed = values * scale
    return scale * (pulled - normed * jnp.mean(normed * pulled, -1, keepdims=True))


def joined(parts):
    return jnp.concatenate(parts, axis=0)


def per_device(
    tokens, cotangent, doc_lengths, attn_gain, w_qkv, w_beta, conv_weight, head_gain,
    w_out, ffn_gain, w_gate_up, w_down,
):
    batches, local_rows, width = tokens.shape
    size = lax.axis_size("tensor")
    dp_size = lax.axis_size("dp")
    slots = local_rows * size
    shard = w_qkv.shape[0]
    heads = w_beta.shape[1]
    units = w_down.shape[0]
    head_share = head_gain.shape[0]
    head_dim = head_share * dp_size
    columns = 3 * heads * head_dim
    conv_share = 12 * heads * head_share
    small_share = conv_share + head_share
    extra = -(-small_share // shard)
    small_at = columns + heads

    attn_column = attn_gain.astype(F32)[:, None]
    ffn_column = ffn_gain.astype(F32)[:, None]
    qkv_rows = jnp.concatenate([w_qkv.reshape(shard, columns), w_beta], axis=1).astype(F32)
    small = jnp.concatenate(
        [conv_weight.reshape(-1), head_gain, jnp.zeros((extra * shard - small_share,), BF16)]
    ).reshape(shard, extra)
    blank = jnp.zeros((shard, LANES - heads - extra), BF16)
    full_proj = gather_dp(
        jnp.concatenate([(attn_column * qkv_rows).astype(BF16), small, blank], axis=1)
    )
    full_out = gather_dp(w_out.T)
    gate_up_rows = w_gate_up.reshape(shard, 2 * units).astype(F32)
    full_gate_up = gather_dp((ffn_column * gate_up_rows).astype(BF16))
    full_down = gather_dp(w_down.T)
    small = full_proj[:, small_at : small_at + extra].astype(F32).reshape(dp_size, extra * shard)
    full_conv = small[:, :conv_share].reshape(dp_size, 12, heads, head_share)
    full_conv = jnp.transpose(full_conv, (1, 2, 0, 3)).reshape(12, heads * head_dim)
    full_head_gain = small[:, conv_share:small_share].reshape(1, head_dim)

    rows = [tokens[index].astype(F32) for index in range(batches)]
    layouts = [doc_layout(doc_lengths[index, 0], slots) for index in range(batches)]

    def mix(index, projected, *beside):
        mixed, *kept = mixer_forward(
            projected, full_conv, full_head_gain, *layouts[index], heads
        )
        return mixed, kept, dot(held(mixed, beside), full_out, 1, 1, BF16)

    def after_mixer(index, branch):
        hidden = rows[index] + branch
        return hidden, (hidden * row_scale(hidden)).astype(BF16)

    def feed(ffn_full):
        gate_up = dot(ffn_full, full_gate_up, 1, 0)
        gate = gate_up[:, :units]
        activated = (gate * sigmoid(gate) * gate_up[:, units:]).astype(BF16)
        return gate_up, activated

    def feed_back(gate_up, cot_full, *beside):
        grad_act = dot(cot_full, full_down, 1, 0)
        gate = gate_up[:, :units]
        up = gate_up[:, units:]
        opened = sigmoid(gate)
        grad_gate = grad_act * up * opened * (1.0 + gate * (1.0 - opened))
        grad_up = grad_act * (gate * opened)
        grad_gate_up = jnp.concatenate([grad_gate, grad_up], axis=1).astype(BF16)
        return grad_gate_up, dot(held(grad_gate_up, beside), full_gate_up, 1, 1, BF16)

    def before_ffn(index, hidden, pulled):
        return cotangent[index].astype(F32) + norm_pull(hidden, pulled)

    def mix_back(index, grad_mixed, projected, kept):
        grad_proj, conv_grad, gain_grad = mixer_backward(
            projected, full_conv, full_head_gain, *layouts[index], heads, kept, grad_mixed
        )
        return grad_proj, conv_grad, gain_grad, dot(grad_proj, full_proj, 1, 1, BF16)

    attn_in = [(rows[index] * row_scale(rows[index])).astype(BF16) for index in range(batches)]
    attn_0, first, last = gather_rows(attn_in[0])
    attn_1, attn_first, _ = gather_rows(attn_in[1], last, full_proj)
    cot_0, cot_first, _ = gather_rows(cotangent[0], last, full_proj)
    proj_0 = dot(attn_0, full_proj, 1, 0)
    mixed_0, kept_0, part_0 = mix(0, proj_0, attn_first, cot_first)

    branch, first, last = scatter_rows(part_0)
    proj_1 = dot(attn_1, full_proj, 1, 0)
    mixed_1, kept_1, part_1 = mix(1, held(proj_1, first), last, cot_0)
    hidden_0, ffn_in = after_mixer(0, branch)

    ffn_0, ffn_first, _ = gather_rows(ffn_in, part_1, full_gate_up)
    branch, first, last = scatter_rows(part_1, ffn_first)
    gate_up_0, act_0 = feed(held(ffn_0, first))
    grad_gate_up_0, part_0 = feed_back(gate_up_0, cot_0, last)
    hidden_1, ffn_in = after_mixer(1, branch)

    ffn_1, ffn_first, _ = gather_rows(ffn_in)
    down_0 = dot(held(act_0, part_0), full_down, 1, 1, BF16)
    down_grad = dot(held(cot_0, down_0), act_0, 0, 0, BF16)
    cot_1, cot_first, _ = gather_rows(cotangent[1], ffn_first)
    pulled, first, last = scatter_rows(part_0, ffn_first)
    gate_up_grad = dot(held(ffn_0, down_grad, ffn_first), grad_gate_up_0, 0, 0, BF16)
    gate_up_1, act_1 = feed(held(ffn_1, first, gate_up_grad))
    grad_gate_up_1, part_1 = feed_back(gate_up_1, cot_1, last)
    grad_hidden_0 = before_ffn(0, hidden_0, pulled)

    branch_0, first, last = gather_rows(grad_hidden_0.astype(BF16))
    pulled, first, last = scatter_rows(part_1, first)
    gate_up_grad = gate_up_grad + dot(held(ffn_1, first, branch_0), grad_gate_up_1, 0, 0)
    gate_up_grad = gate_up_grad.astype(BF16)
    grad_hidden_1 = before_ffn(1, hidden_1, pulled)

    branch_in = held(grad_hidden_1.astype(BF16), gate_up_grad)
    branch_1, branch_first, last = gather_rows(branch_in)
    gate_up_grad = scatter_dp(gate_up_grad)
    grad_mixed = dot(held(branch_0, branch_in), full_out, 1, 0)
    grad_proj_0, conv_grad_0, gain_grad_0, part_0 = mix_back(0, grad_mixed, proj_0, kept_0)
    lower_0, down_first, down_last = scatter_rows(down_0, branch_in, mid=(part_0,))
    act_1_held = held(act_1, part_0, branch_first)
    down_1 = dot(act_1_held, full_down, 1, 1, BF16)
    down_grad = (down_grad + dot(cot_1, act_1_held, 0, 0)).astype(BF16)

    pulled, first, last = scatter_rows(part_0, last)
    out_grad = dot(
        joined([held(branch_0, part_0), branch_1]), joined([mixed_0, mixed_1]), 0, 0, BF16
    )
    grad_mixed = dot(held(branch_1, part_0), full_out, 1, 0)
    input_rows_0 = grad_hidden_0 + norm_pull(rows[0], pulled)
    grad_mixed = held(grad_mixed, first, down_first, out_grad, down_1, down_grad)
    down_grad = scatter_dp(down_grad)
    grad_proj_1, conv_grad_1, gain_grad_1, part_1 = mix_back(1, grad_mixed, proj_1, kept_1)

    attn_all = joined([held(attn_0, part_1, last, down_last), attn_1])
    pulled, first, last = scatter_rows(part_1, last, down_last)
    proj_grad = dot(attn_all, joined([grad_proj_0, grad_proj_1]), 0, 0, BF16)
    conv_grad = (conv_grad_0 + conv_grad_1).reshape(12, heads, dp_size, head_share)
    conv_grad = jnp.transpose(conv_grad, (2, 0, 1, 3)).reshape(dp_size, conv_share)
    head_gain_grad = (gain_grad_0 + gain_grad_1).reshape(dp_size, head_share)
    small_grad = jnp.concatenate(
        [conv_grad, head_gain_grad, jnp.zeros((dp_size, extra * shard - small_share), F32)], axis=1
    )
    small_grad = small_grad.reshape(dp_size * shard, extra).astype(BF16)
    small_grad = jnp.pad(small_grad, ((0, 0), (small_at, LANES - heads - extra)))
    mixer_grad = scatter_dp(jnp.concatenate([proj_grad + small_grad, out_grad], axis=1))
    lower_1, first, last = scatter_rows(down_1, last, mid=(gate_up_grad,))
    mixer_grad = held(mixer_grad, last)
    input_rows_1 = grad_hidden_1 + norm_pull(rows[1], pulled)
    layer_rows_0 = (hidden_0 + lower_0).astype(BF16)
    layer_rows_1 = (hidden_1 + lower_1).astype(BF16)

    proj_grad = mixer_grad[:, : columns + LANES].astype(F32)
    out_grad = mixer_grad[:, columns + LANES :]
    gate_up_grad = gate_up_grad.astype(F32)
    small_grad = proj_grad[:, small_at : small_at + extra].reshape(extra * shard)
    gain_grads = jnp.concatenate(
        [
            jnp.sum(proj_grad[:, :small_at] * qkv_rows, axis=1),
            jnp.sum(gate_up_grad * gate_up_rows, axis=1),
            small_grad[conv_share:small_share],
        ]
    )[None]
    total = gain_grads
    for step in range(1, size):
        total = total + ring_shift(gain_grads, step)
    total = total[0]
    proj_grad = proj_grad[:, :small_at] * attn_column
    return (
        jnp.stack([layer_rows_0, layer_rows_1]),
        jnp.stack([input_rows_0, input_rows_1]),
        total[:shard],
        proj_grad[:, :columns].reshape(shard, 3, -1),
        proj_grad[:, columns:],
        small_grad[:conv_share].reshape(3, 4, heads, head_share),
        total[2 * shard :],
        out_grad.T.astype(F32),
        total[shard : 2 * shard],
        (gate_up_grad * ffn_column).reshape(shard, 2, units),
        down_grad.T.astype(F32),
    )


def solution(mesh):
    return jax.shard_map(
        per_device,
        mesh=mesh,
        in_specs=(
            P(None, ("dp", "tensor"), None),
            P(None, ("dp", "tensor"), None),
            P(None, "dp", None),
            P("dp"),
            P("dp", None, "tensor"),
            P("dp", "tensor"),
            P(None, None, "tensor", "dp"),
            P("dp"),
            P("tensor", "dp"),
            P("dp"),
            P("dp", None, "tensor"),
            P("tensor", "dp"),
        ),
        out_specs=(
            P(None, ("dp", "tensor"), None),
            P(None, ("dp", "tensor"), None),
            P("dp"),
            P("dp", None, "tensor"),
            P("dp", "tensor"),
            P(None, None, "tensor", "dp"),
            P("dp"),
            P("tensor", "dp"),
            P("dp"),
            P("dp", None, "tensor"),
            P("tensor", "dp"),
        ),
        check_vma=False,
    )
```

```python
import jax
import jax.numpy as jnp
from jax import lax
from jax.experimental import pallas as pl
from jax.experimental.pallas import tpu as pltpu
from jax.sharding import PartitionSpec as P

BLOCK = 64
NORM_EPS = 1e-06
HEAD_EPS = 1e-05
F32 = jnp.float32
BF16 = jnp.bfloat16
LANES = 128
HALO = 8


def low_dot(left, right, left_dim, right_dim):
    return lax.dot_general(
        left.astype(BF16),
        right.astype(BF16),
        (((left_dim,), (right_dim,)), ((), ())),
        preferred_element_type=F32,
    )


def sigmoid(value):
    return 1.0 / (1.0 + jnp.exp(-value))


def block_masks(rows):
    row = lax.broadcasted_iota(jnp.int32, (rows, rows), 0)
    col = lax.broadcasted_iota(jnp.int32, (rows, rows), 1)
    same = {size: (row // size) == (col // size) for size in (8, 16, 32, 64)}
    strict = jnp.logical_and(same[64], col < row)
    lower = jnp.logical_and(same[64], col <= row)
    eye = (row == col).astype(F32)
    return same, strict, lower, eye


def unit_inverse(system, same, eye):
    base = jnp.where(same[8], system, 0.0)
    square = low_dot(base, base, 1, 0)
    fourth = low_dot(square, square, 1, 0)
    inverse = eye - base
    inverse = inverse + low_dot(inverse, square, 1, 0)
    inverse = inverse + low_dot(inverse, fourth, 1, 0)
    for size in (8, 16, 32):
        off = jnp.where(jnp.logical_and(same[2 * size], jnp.logical_not(same[size])), system, 0.0)
        inverse = inverse - low_dot(inverse, low_dot(off, inverse, 1, 0), 1, 0)
    return inverse


def delayed_rows(previous, current, lag):
    if lag == 0:
        return current
    rows = current.shape[0]
    joined = jnp.concatenate([previous, current], axis=0)
    return joined[HALO - lag : HALO - lag + rows]


def conv_part(proj_ref, before_ref, conv_ref, reach, part, head, head_dim, heads):
    width = heads * head_dim
    column = part * width + head * head_dim
    current = proj_ref[:, column : column + head_dim]
    previous = before_ref[:, column : column + head_dim]
    taps = [conv_ref[part * 4 + lag : part * 4 + lag + 1, head * head_dim : (head + 1) * head_dim] for lag in range(4)]
    shifted = [current]
    for lag in range(1, 4):
        shifted.append(delayed_rows(previous, current, lag) * reach[lag])
    total = taps[0] * shifted[0]
    for lag in range(1, 4):
        total = total + taps[lag] * shifted[lag]
    return total, shifted, taps


def stack_heads(pieces, index):
    return jnp.concatenate([piece[index * BLOCK : (index + 1) * BLOCK] for piece in pieces], axis=0)


def forward_kernel(
    proj_ref, before_ref, logit_ref, pos_ref, valid_ref, conv_ref, gain_ref,
    mixed_ref, recall_ref, start_ref, inverse_ref, update_ref, weight_ref,
    state_ref, *, heads, head_dim,
):
    rows = proj_ref.shape[0]
    blocks = rows // BLOCK
    stacked = heads * BLOCK

    @pl.when(pl.program_id(0) == 0)
    def _():
        state_ref[...] = jnp.zeros_like(state_ref)

    pos = pos_ref[...]
    valid = valid_ref[...]
    reach = [None] + [(pos >= lag).astype(F32) for lag in range(1, 4)]
    parts = [[], [], []]
    strengths = []
    for head in range(heads):
        for part in range(3):
            total, _, _ = conv_part(proj_ref, before_ref, conv_ref, reach, part, head, head_dim, heads)
            value = total * sigmoid(total)
            if part < 2:
                scale = lax.rsqrt(jnp.sum(value * value, -1, keepdims=True) + NORM_EPS)
                if part == 0:
                    scale = scale * head_dim ** (-0.5)
                value = value * scale
            parts[part].append(value)
        strengths.append(sigmoid(logit_ref[:, head : head + 1]) * valid)
    same, strict, lower, eye = block_masks(stacked)
    local = []
    for index in range(blocks):
        queries = stack_heads(parts[0], index).astype(BF16)
        keys = stack_heads(parts[1], index)
        values = stack_heads(parts[2], index)
        strength = stack_heads(strengths, index)
        keys_low = keys.astype(BF16)
        gram = low_dot(keys_low, keys_low, 1, 1)
        system = jnp.where(strict, strength * gram, 0.0)
        inverse = unit_inverse(system, same, eye).astype(BF16)
        weighted = low_dot(inverse, strength * keys, 1, 0).astype(BF16)
        fresh = low_dot(inverse, strength * values, 1, 0)
        scores = jnp.where(lower, low_dot(queries, keys_low, 1, 1), 0.0).astype(BF16)
        inverse_ref[index] = inverse
        weight_ref[index] = weighted
        local.append((queries, keys_low, weighted, fresh, scores))
    for index in range(blocks):
        queries, keys_low, weighted, fresh, scores = local[index]
        keep = (pos[index * BLOCK : index * BLOCK + 1] != 0).astype(F32)
        updates = []
        carried = []
        for head in range(heads):
            span = slice(head * BLOCK, (head + 1) * BLOCK)
            state = state_ref[head] * keep
            state_low = state.astype(BF16)
            start_ref[index, head] = state_low
            update = fresh[span] - low_dot(weighted[span], state_low, 1, 1)
            update_low = update.astype(BF16)
            updates.append(update_low)
            carried.append(low_dot(queries[span], state_low, 1, 1))
            state_ref[head] = state + low_dot(update_low, keys_low[span], 0, 0)
        update_all = jnp.concatenate(updates, axis=0)
        update_ref[index] = update_all
        recall_all = jnp.concatenate(carried, axis=0) + low_dot(scores, update_all, 1, 0)
        scale = lax.rsqrt(jnp.mean(recall_all * recall_all, -1, keepdims=True) + HEAD_EPS)
        normed = recall_all * scale * gain_ref[...]
        here = slice(index * BLOCK, (index + 1) * BLOCK)
        for head in range(heads):
            span = slice(head * BLOCK, (head + 1) * BLOCK)
            column = slice(head * head_dim, (head + 1) * head_dim)
            recall_ref[here, column] = recall_all[span]
            mixed_ref[here, column] = (normed[span] * valid[here]).astype(BF16)


def backward_kernel(
    proj_ref, before_ref, logit_ref, pos_ref, after_ref, valid_ref, conv_ref, gain_ref,
    recall_ref, start_ref, inverse_ref, update_ref, weight_ref, mixed_grad_ref,
    proj_grad_ref, conv_grad_ref, gain_grad_ref,
    state_ref, halo_ref, *, heads, head_dim,
):
    rows = proj_ref.shape[0]
    blocks = rows // BLOCK
    stacked = heads * BLOCK
    width = heads * head_dim

    @pl.when(pl.program_id(0) == 0)
    def _():
        state_ref[...] = jnp.zeros_like(state_ref)
        halo_ref[...] = jnp.zeros_like(halo_ref)
        conv_grad_ref[...] = jnp.zeros_like(conv_grad_ref)
        gain_grad_ref[...] = jnp.zeros_like(gain_grad_ref)

    pos = pos_ref[...]
    valid = valid_ref[...]
    reach = [None] + [(pos >= lag).astype(F32) for lag in range(1, 4)]
    pos_ahead = jnp.concatenate([pos, after_ref[...]], axis=0)
    reach_ahead = [None] + [(pos_ahead >= lag).astype(F32) for lag in range(1, 4)]
    gain = gain_ref[...]
    parts = [[], [], []]
    gates = []
    recall_grads = []
    gain_grad = jnp.zeros((1, head_dim), F32)
    for head in range(heads):
        for part in range(3):
            total, _, _ = conv_part(proj_ref, before_ref, conv_ref, reach, part, head, head_dim, heads)
            value = total * sigmoid(total)
            if part < 2:
                scale = lax.rsqrt(jnp.sum(value * value, -1, keepdims=True) + NORM_EPS)
                if part == 0:
                    scale = scale * head_dim ** (-0.5)
                value = value * scale
            parts[part].append(value)
        gates.append(sigmoid(logit_ref[:, head : head + 1]))
        column = slice(head * head_dim, (head + 1) * head_dim)
        recall = recall_ref[:, column]
        pulled = mixed_grad_ref[:, column] * valid
        scale = lax.rsqrt(jnp.mean(recall * recall, -1, keepdims=True) + HEAD_EPS)
        normed = recall * scale
        gain_grad = gain_grad + jnp.sum(pulled * normed, 0, keepdims=True)
        pulled = pulled * gain
        recall_grads.append(
            scale * (pulled - normed * jnp.mean(normed * pulled, -1, keepdims=True))
        )
    gain_grad_ref[...] += gain_grad
    strengths = [gate * valid for gate in gates]
    same, strict, lower, eye = block_masks(stacked)
    query_grads = [None] * blocks
    key_grads = [None] * blocks
    value_grads = [None] * blocks
    strength_grads = [None] * blocks
    for index in range(blocks - 1, -1, -1):
        queries = stack_heads(parts[0], index).astype(BF16)
        keys = stack_heads(parts[1], index).astype(BF16)
        values = stack_heads(parts[2], index)
        strength = stack_heads(strengths, index)
        out_grad = stack_heads(recall_grads, index).astype(BF16)
        inverse = inverse_ref[index]
        weighted = weight_ref[index]
        update = update_ref[index]
        gram = low_dot(keys, keys, 1, 1)
        scores = jnp.where(lower, low_dot(queries, keys, 1, 1), 0.0).astype(BF16)
        local_grad = low_dot(scores, out_grad, 0, 0)
        score_grad = jnp.where(lower, low_dot(out_grad, update, 1, 1), 0.0).astype(BF16)
        keep = (pos[index * BLOCK : index * BLOCK + 1] != 0).astype(F32)
        update_grads = []
        query_carried = []
        key_carried = []
        misses = []
        starts = []
        for head in range(heads):
            span = slice(head * BLOCK, (head + 1) * BLOCK)
            ahead = state_ref[head]
            ahead_low = ahead.astype(BF16)
            start = start_ref[index, head]
            starts.append(start)
            update_grad = local_grad[span] + low_dot(keys[span], ahead_low, 1, 1)
            update_grad_low = update_grad.astype(BF16)
            update_grads.append(update_grad_low)
            carried = ahead + low_dot(out_grad[span], queries[span], 0, 0)
            carried = carried - low_dot(update_grad_low, weighted[span], 0, 0)
            state_ref[head] = carried * keep
            query_carried.append(low_dot(out_grad[span], start, 1, 0))
            key_carried.append(low_dot(update[span], ahead_low, 1, 0))
            misses.append(values[span] - low_dot(keys[span], start, 1, 1))
        miss_grad = low_dot(inverse, jnp.concatenate(update_grads, axis=0), 0, 0)
        miss = jnp.concatenate(misses, axis=0)
        system_grad = jnp.where(strict, -low_dot(miss_grad, update, 1, 1), 0.0)
        strength_grads[index] = jnp.sum(miss_grad * miss, -1, keepdims=True) + jnp.sum(
            system_grad * gram, -1, keepdims=True
        )
        gram_grad = (strength * system_grad).astype(BF16)
        value_grad = strength * miss_grad
        value_low = value_grad.astype(BF16)
        value_grads[index] = value_grad
        query_grads[index] = jnp.concatenate(query_carried, axis=0) + low_dot(score_grad, keys, 1, 0)
        key_grad = jnp.concatenate(key_carried, axis=0) + low_dot(score_grad, queries, 0, 0)
        key_grad = key_grad + low_dot(gram_grad, keys, 1, 0) + low_dot(gram_grad, keys, 0, 0)
        key_state = [
            low_dot(value_low[head * BLOCK : (head + 1) * BLOCK], starts[head], 1, 0)
            for head in range(heads)
        ]
        key_grads[index] = key_grad - jnp.concatenate(key_state, axis=0)
    grads = [query_grads, key_grads, value_grads]
    logit_grads = []
    for head in range(heads):
        span = slice(head * BLOCK, (head + 1) * BLOCK)
        gate = gates[head]
        pulled = jnp.concatenate([strength_grads[index][span] for index in range(blocks)], axis=0)
        logit_grads.append(pulled * valid * gate * (1.0 - gate))
        for part in range(3):
            pulled = jnp.concatenate([grads[part][index][span] for index in range(blocks)], axis=0)
            total, shifted, taps = conv_part(
                proj_ref, before_ref, conv_ref, reach, part, head, head_dim, heads
            )
            gate_part = sigmoid(total)
            value = total * gate_part
            if part < 2:
                scale = lax.rsqrt(jnp.sum(value * value, -1, keepdims=True) + NORM_EPS)
                normed = value * scale
                pulled = scale * (pulled - normed * jnp.sum(normed * pulled, -1, keepdims=True))
                if part == 0:
                    pulled = pulled * head_dim ** (-0.5)
            pre_grad = pulled * gate_part * (1.0 + total * (1.0 - gate_part))
            column = slice(part * width + head * head_dim, part * width + (head + 1) * head_dim)
            tap_column = slice(head * head_dim, (head + 1) * head_dim)
            for lag in range(4):
                conv_grad_ref[part * 4 + lag : part * 4 + lag + 1, tap_column] += jnp.sum(
                    pre_grad * shifted[lag], 0, keepdims=True
                )
            joined = jnp.concatenate([pre_grad, halo_ref[:, column]], axis=0)
            total_grad = taps[0] * pre_grad
            for lag in range(1, 4):
                total_grad = total_grad + taps[lag] * (joined * reach_ahead[lag])[lag : lag + rows]
            proj_grad_ref[:, column] = total_grad.astype(BF16)
            halo_ref[:, column] = pre_grad[:HALO]
    blank = jnp.zeros((rows, LANES - heads), F32)
    proj_grad_ref[:, 3 * width :] = jnp.concatenate(logit_grads + [blank], axis=1).astype(BF16)


def mixer_specs(rows, columns, order):
    blocks = rows // BLOCK
    ratio = rows // HALO

    def whole(*shape):
        return pl.BlockSpec(shape, lambda step: (0,) * len(shape))

    def by_rows(size, column=0):
        return pl.BlockSpec((rows, size), lambda step: (order(step), column))

    def by_blocks(*tail):
        return pl.BlockSpec((blocks,) + tail, lambda step: (order(step),) + (0,) * len(tail))

    before = pl.BlockSpec(
        (HALO, columns), lambda step: (jnp.maximum(order(step) * ratio - 1, 0), 0)
    )
    return whole, by_rows, by_blocks, before


def mixer_forward(projected, conv_rows, head_gain, pos, valid, heads):
    slots = projected.shape[0]
    head_dim = head_gain.shape[1]
    width = heads * head_dim
    columns = 3 * width
    rows = slots // lax.axis_size("tensor")
    steps = slots // rows
    stacked = heads * BLOCK
    block_count = slots // BLOCK
    whole, by_rows, by_blocks, before = mixer_specs(rows, columns, lambda step: step)
    return pl.pallas_call(
        lambda *refs: forward_kernel(*refs, heads=heads, head_dim=head_dim),
        grid=(steps,),
        in_specs=[
            by_rows(columns),
            before,
            by_rows(LANES, columns // LANES),
            by_rows(1),
            by_rows(1),
            whole(12, width),
            whole(1, head_dim),
        ],
        out_specs=[
            by_rows(width),
            by_rows(width),
            by_blocks(heads, head_dim, head_dim),
            by_blocks(stacked, stacked),
            by_blocks(stacked, head_dim),
            by_blocks(stacked, head_dim),
        ],
        scratch_shapes=[pltpu.VMEM((heads, head_dim, head_dim), F32)],
        out_shape=[
            jax.ShapeDtypeStruct((slots, width), BF16),
            jax.ShapeDtypeStruct((slots, width), F32),
            jax.ShapeDtypeStruct((block_count, heads, head_dim, head_dim), BF16),
            jax.ShapeDtypeStruct((block_count, stacked, stacked), BF16),
            jax.ShapeDtypeStruct((block_count, stacked, head_dim), BF16),
            jax.ShapeDtypeStruct((block_count, stacked, head_dim), BF16),
        ],
        name="mixer_forward",
    )(projected, projected, projected, pos, valid, conv_rows, head_gain)


def mixer_backward(projected, conv_rows, head_gain, pos, valid, heads, kept, mixed_grad):
    slots = projected.shape[0]
    head_dim = head_gain.shape[1]
    width = heads * head_dim
    columns = 3 * width
    rows = slots // lax.axis_size("tensor")
    steps = slots // rows
    stacked = heads * BLOCK
    ratio = rows // HALO
    recall, start, inverse, update, weighted = kept
    pos_padded = jnp.pad(pos, ((0, HALO), (0, 0)))
    whole, by_rows, by_blocks, before = mixer_specs(rows, columns, lambda step: steps - 1 - step)
    return pl.pallas_call(
        lambda *refs: backward_kernel(*refs, heads=heads, head_dim=head_dim),
        grid=(steps,),
        in_specs=[
            by_rows(columns),
            before,
            by_rows(LANES, columns // LANES),
            by_rows(1),
            pl.BlockSpec((HALO, 1), lambda step: ((steps - step) * ratio, 0)),
            by_rows(1),
            whole(12, width),
            whole(1, head_dim),
            by_rows(width),
            by_blocks(heads, head_dim, head_dim),
            by_blocks(stacked, stacked),
            by_blocks(stacked, head_dim),
            by_blocks(stacked, head_dim),
            by_rows(width),
        ],
        out_specs=[by_rows(columns + LANES), whole(12, width), whole(1, head_dim)],
        scratch_shapes=[
            pltpu.VMEM((heads, head_dim, head_dim), F32),
            pltpu.VMEM((HALO, columns), F32),
        ],
        out_shape=[
            jax.ShapeDtypeStruct((slots, columns + LANES), BF16),
            jax.ShapeDtypeStruct((12, width), F32),
            jax.ShapeDtypeStruct((1, head_dim), F32),
        ],
        name="mixer_backward",
    )(
        projected, projected, projected, pos, pos_padded, valid, conv_rows, head_gain,
        recall, start, inverse, update, weighted, mixed_grad,
    )


def doc_layout(length_pair, slot_count):
    first_end = (length_pair[0] + BLOCK - 1) // BLOCK * BLOCK
    second_end = first_end + (length_pair[1] + BLOCK - 1) // BLOCK * BLOCK
    places = jnp.arange(slot_count, dtype=jnp.int32)
    in_first = places < first_end
    in_second = jnp.logical_and(places >= first_end, places < second_end)
    doc_begin = jnp.where(in_first, 0, jnp.where(in_second, first_end, second_end))
    doc_limit = jnp.where(in_first, length_pair[0], jnp.where(in_second, length_pair[1], 0))
    offset = places - doc_begin
    is_valid = (offset < doc_limit).astype(F32)
    return offset.astype(F32)[:, None], is_valid[:, None]


def ring_shift(value, step):
    size = lax.axis_size("tensor")
    return lax.ppermute(value, "tensor", [(place, (place + step) % size) for place in range(size)])


def held(value, *others):
    return lax.optimization_barrier((value, others))[0]


def piece_start(step, count):
    size = lax.axis_size("tensor")
    return lax.rem(lax.axis_index("tensor") + step, size) * count


def gather_rows(rows, *token, mid=()):
    size = lax.axis_size("tensor")
    count = rows.shape[0]
    half = count // 2
    rows = held(rows, token)
    full = jnp.zeros((size * count, rows.shape[1]), rows.dtype)

    def put(full, piece, step, at=0):
        return lax.dynamic_update_slice(full, piece, (piece_start(step, count) + at, 0))

    full = put(full, rows, 0)
    from_left = rows
    from_right = rows
    for step in range(1, size // 2):
        from_left = ring_shift(from_left, 1)
        from_right = ring_shift(from_right, -1)
        full = put(full, from_left, size - step)
        full = put(full, from_right, step)
    from_left_half, from_right_half = from_left[:half], from_right[half:]
    if mid:
        from_left_half, from_right_half = held((from_left_half, from_right_half), mid)
    far = ring_shift(from_left_half, 1), ring_shift(from_right_half, -1)
    full = put(full, far[0], size // 2)
    full = put(full, far[1], size // 2, half)
    return full, (from_left, from_right), far


def ring_rows(low, step, at, length):
    count = low.shape[0] // lax.axis_size("tensor")
    start = piece_start(step, count) + at
    return lax.dynamic_slice(low, (start, 0), (length, low.shape[1])).astype(F32)


def scatter_rows_begin(partial, *token):
    size = lax.axis_size("tensor")
    half = partial.shape[0] // size // 2
    low = held(partial, token)
    to_right = ring_shift(ring_rows(low, size // 2, 0, half).astype(BF16), 1)
    to_left = ring_shift(ring_rows(low, size // 2, half, half).astype(BF16), -1)
    return low, (to_right, to_left)


def scatter_rows_end(state, *token):
    size = lax.axis_size("tensor")
    low, (to_right, to_left) = state
    count = low.shape[0] // size
    half = count // 2
    if token:
        to_right, to_left = held((to_right, to_left), token)
    for step in range(size // 2 - 1, 0, -1):
        right = ring_rows(low, step, 0, count)
        left = ring_rows(low, size - step, 0, count)
        if step == size // 2 - 1:
            right = joined([right[:half] + to_right.astype(F32), right[half:]])
            left = joined([left[:half], left[half:] + to_left.astype(F32)])
        else:
            right = right + to_right.astype(F32)
            left = left + to_left.astype(F32)
        to_right = ring_shift(right.astype(BF16), 1)
        to_left = ring_shift(left.astype(BF16), -1)
    total = ring_rows(low, 0, 0, count) + to_right.astype(F32) + to_left.astype(F32)
    return total, (to_right, to_left)


def scatter_rows(partial, *token, mid=()):
    state = scatter_rows_begin(partial, *token)
    total, last = scatter_rows_end(state, *mid)
    return total, state[1], last


def dot(left, right, left_dim, right_dim, out_type=F32):
    return lax.dot_general(
        left, right, (((left_dim,), (right_dim,)), ((), ())), preferred_element_type=out_type
    )


def gather_dp(value):
    return lax.all_gather(value, "dp", axis=0, tiled=True)


def scatter_dp(value):
    return lax.psum_scatter(value, "dp", scatter_dimension=0, tiled=True)


def row_scale(values):
    return lax.rsqrt(jnp.mean(values * values, -1, keepdims=True) + NORM_EPS)


def norm_pull(values, pulled):
    scale = row_scale(values)
    normed = values * scale
    return scale * (pulled - normed * jnp.mean(normed * pulled, -1, keepdims=True))


def joined(parts):
    return jnp.concatenate(parts, axis=0)


def per_device(
    tokens, cotangent, doc_lengths, attn_gain, w_qkv, w_beta, conv_weight, head_gain,
    w_out, ffn_gain, w_gate_up, w_down,
):
    batches, local_rows, width = tokens.shape
    size = lax.axis_size("tensor")
    dp_size = lax.axis_size("dp")
    slots = local_rows * size
    shard = w_qkv.shape[0]
    heads = w_beta.shape[1]
    units = w_down.shape[0]
    head_share = head_gain.shape[0]
    head_dim = head_share * dp_size
    columns = 3 * heads * head_dim
    conv_share = 12 * heads * head_share
    small_share = conv_share + head_share
    extra = -(-small_share // shard)
    small_at = columns + heads

    attn_column = attn_gain.astype(F32)[:, None]
    ffn_column = ffn_gain.astype(F32)[:, None]
    qkv_rows = jnp.concatenate([w_qkv.reshape(shard, columns), w_beta], axis=1).astype(F32)
    small = jnp.concatenate(
        [conv_weight.reshape(-1), head_gain, jnp.zeros((extra * shard - small_share,), BF16)]
    ).reshape(shard, extra)
    blank = jnp.zeros((shard, LANES - heads - extra), BF16)
    full_proj = gather_dp(
        jnp.concatenate([(attn_column * qkv_rows).astype(BF16), small, blank], axis=1)
    )
    full_out = gather_dp(w_out.T)
    gate_up_rows = w_gate_up.reshape(shard, 2 * units).astype(F32)
    full_gate_up = gather_dp((ffn_column * gate_up_rows).astype(BF16))
    full_down = gather_dp(w_down.T)
    small = full_proj[:, small_at : small_at + extra].astype(F32).reshape(dp_size, extra * shard)
    full_conv = small[:, :conv_share].reshape(dp_size, 12, heads, head_share)
    full_conv = jnp.transpose(full_conv, (1, 2, 0, 3)).reshape(12, heads * head_dim)
    full_head_gain = small[:, conv_share:small_share].reshape(1, head_dim)

    rows = [tokens[index].astype(F32) for index in range(batches)]
    layouts = [doc_layout(doc_lengths[index, 0], slots) for index in range(batches)]

    def mix(index, projected, *beside):
        mixed, *kept = mixer_forward(
            projected, full_conv, full_head_gain, *layouts[index], heads
        )
        return mixed, kept, dot(held(mixed, beside), full_out, 1, 1, BF16)

    def after_mixer(index, branch):
        hidden = rows[index] + branch
        return hidden, (hidden * row_scale(hidden)).astype(BF16)

    def feed(ffn_full):
        gate_up = dot(ffn_full, full_gate_up, 1, 0)
        gate = gate_up[:, :units]
        activated = (gate * sigmoid(gate) * gate_up[:, units:]).astype(BF16)
        return gate_up, activated

    def feed_back(gate_up, cot_full, *beside):
        grad_act = dot(cot_full, full_down, 1, 0)
        gate = gate_up[:, :units]
        up = gate_up[:, units:]
        opened = sigmoid(gate)
        grad_gate = grad_act * up * opened * (1.0 + gate * (1.0 - opened))
        grad_up = grad_act * (gate * opened)
        grad_gate_up = jnp.concatenate([grad_gate, grad_up], axis=1).astype(BF16)
        return grad_gate_up, dot(held(grad_gate_up, beside), full_gate_up, 1, 1, BF16)

    def before_ffn(index, hidden, pulled):
        return cotangent[index].astype(F32) + norm_pull(hidden, pulled)

    attn_in = [(rows[index] * row_scale(rows[index])).astype(BF16) for index in range(batches)]
    attn_0, first, last = gather_rows(attn_in[0])
    attn_1, attn_first, _ = gather_rows(attn_in[1], last, full_proj)
    cot_0, cot_first, _ = gather_rows(cotangent[0], last, full_proj)
    proj_0 = dot(attn_0, full_proj, 1, 0)
    mixed_0, kept_0, part_0 = mix(0, proj_0, attn_first, cot_first)

    branch, first, last = scatter_rows(part_0)
    proj_1 = dot(attn_1, full_proj, 1, 0)
    mixed_1, kept_1, part_1 = mix(1, held(proj_1, first), last, cot_0)
    hidden_0, ffn_in = after_mixer(0, branch)

    ffn_0, ffn_first, _ = gather_rows(ffn_in, part_1, full_gate_up)
    branch, first, last = scatter_rows(part_1, ffn_first)
    gate_up_0, act_0 = feed(held(ffn_0, first))
    grad_gate_up_0, part_0 = feed_back(gate_up_0, cot_0, last)
    hidden_1, ffn_in = after_mixer(1, branch)

    ffn_1, ffn_first, _ = gather_rows(ffn_in)
    down_0 = dot(held(act_0, part_0), full_down, 1, 1, BF16)
    down_grad = dot(held(cot_0, down_0), act_0, 0, 0, BF16)
    cot_1, cot_first, _ = gather_rows(cotangent[1], ffn_first)
    pulled, first, last = scatter_rows(part_0, ffn_first)
    gate_up_grad = dot(held(ffn_0, down_grad, ffn_first), grad_gate_up_0, 0, 0, BF16)
    gate_up_1, act_1 = feed(held(ffn_1, first, gate_up_grad))
    down_state = scatter_rows_begin(down_0, first)
    grad_gate_up_1, part_1 = feed_back(gate_up_1, cot_1, last, down_state[1])
    grad_hidden_0 = before_ffn(0, hidden_0, pulled)

    branch_0, first, last = gather_rows(grad_hidden_0.astype(BF16))
    down_grad = (down_grad + dot(held(cot_1, part_1, first), act_1, 0, 0)).astype(BF16)
    pulled, first, last = scatter_rows(part_1, first)
    gate_up_grad = gate_up_grad + dot(held(ffn_1, first, branch_0, down_grad), grad_gate_up_1, 0, 0)
    gate_up_grad = gate_up_grad.astype(BF16)
    grad_hidden_1 = before_ffn(1, hidden_1, pulled)

    branch_in = held(grad_hidden_1.astype(BF16), gate_up_grad)
    branch_1, branch_first, _ = gather_rows(branch_in)
    down_grad = scatter_dp(down_grad)
    gate_up_grad = scatter_dp(gate_up_grad)
    down_1 = dot(held(act_1, branch_in), full_down, 1, 1, BF16)
    grad_mixed = dot(held(branch_0, branch_in), full_out, 1, 0)
    grad_mixed = held(grad_mixed, branch_first, down_1)
    grad_proj_0, conv_grad_0, gain_grad_0 = mixer_backward(
        proj_0, full_conv, full_head_gain, *layouts[0], heads, kept_0, grad_mixed
    )
    lower_0, down_last = scatter_rows_end(down_state, branch_first)
    part_0 = dot(held(grad_proj_0, branch_1, down_last), full_proj, 1, 1, BF16)

    pulled, first, last = scatter_rows(part_0)
    out_grad = dot(
        joined([held(branch_0, part_0), branch_1]), joined([mixed_0, mixed_1]), 0, 0, BF16
    )
    grad_mixed = dot(held(branch_1, part_0), full_out, 1, 0)
    input_rows_0 = grad_hidden_0 + norm_pull(rows[0], pulled)
    grad_mixed = held(grad_mixed, first, out_grad)
    out_grad = scatter_dp(out_grad)
    grad_proj_1, conv_grad_1, gain_grad_1 = mixer_backward(
        proj_1, full_conv, full_head_gain, *layouts[1], heads, kept_1, grad_mixed
    )
    part_1 = dot(held(grad_proj_1, last), full_proj, 1, 1, BF16)
    attn_all = joined([held(attn_0, last), attn_1])
    pulled, first, last = scatter_rows(part_1, last, down_grad, gate_up_grad)
    down_out = down_grad.T.astype(F32)
    proj_grad = dot(attn_all, joined([grad_proj_0, grad_proj_1]), 0, 0, BF16)
    conv_grad = (conv_grad_0 + conv_grad_1).reshape(12, heads, dp_size, head_share)
    conv_grad = jnp.transpose(conv_grad, (2, 0, 1, 3)).reshape(dp_size, conv_share)
    head_gain_grad = (gain_grad_0 + gain_grad_1).reshape(dp_size, head_share)
    small_grad = jnp.concatenate(
        [conv_grad, head_gain_grad, jnp.zeros((dp_size, extra * shard - small_share), F32)], axis=1
    )
    small_grad = small_grad.reshape(dp_size * shard, extra).astype(BF16)
    small_grad = jnp.pad(small_grad, ((0, 0), (small_at, LANES - heads - extra)))
    proj_grad = scatter_dp(proj_grad + small_grad)
    gate_up_grad = gate_up_grad.astype(F32)
    gate_up_out = (gate_up_grad * ffn_column).reshape(shard, 2, units)
    ffn_gain_grad = jnp.sum(gate_up_grad * gate_up_rows, axis=1)
    out_out = out_grad.T.astype(F32)
    lower_1, first, last = scatter_rows(
        down_1, last, down_out, mid=(gate_up_out, ffn_gain_grad, out_out)
    )
    proj_grad = held(proj_grad, first)
    input_rows_1 = grad_hidden_1 + norm_pull(rows[1], pulled)
    layer_rows_0 = (hidden_0 + lower_0).astype(BF16)
    layer_rows_1 = (hidden_1 + lower_1).astype(BF16)

    proj_grad = proj_grad.astype(F32)
    small_grad = proj_grad[:, small_at : small_at + extra].reshape(extra * shard)
    gain_grads = jnp.concatenate(
        [
            jnp.sum(proj_grad[:, :small_at] * qkv_rows, axis=1),
            ffn_gain_grad,
            small_grad[conv_share:small_share],
        ]
    )[None]
    gain_grads = held(gain_grads, last)
    total = gain_grads
    for step in range(1, size):
        total = total + ring_shift(gain_grads, step)
    total = total[0]
    proj_grad = proj_grad[:, :small_at] * attn_column
    return (
        jnp.stack([layer_rows_0, layer_rows_1]),
        jnp.stack([input_rows_0, input_rows_1]),
        total[:shard],
        proj_grad[:, :columns].reshape(shard, 3, -1),
        proj_grad[:, columns:],
        small_grad[:conv_share].reshape(3, 4, heads, head_share),
        total[2 * shard :],
        out_out,
        total[shard : 2 * shard],
        gate_up_out,
        down_out,
    )


def solution(mesh):
    return jax.shard_map(
        per_device,
        mesh=mesh,
        in_specs=(
            P(None, ("dp", "tensor"), None),
            P(None, ("dp", "tensor"), None),
            P(None, "dp", None),
            P("dp"),
            P("dp", None, "tensor"),
            P("dp", "tensor"),
            P(None, None, "tensor", "dp"),
            P("dp"),
            P("tensor", "dp"),
            P("dp"),
            P("dp", None, "tensor"),
            P("tensor", "dp"),
        ),
        out_specs=(
            P(None, ("dp", "tensor"), None),
            P(None, ("dp", "tensor"), None),
            P("dp"),
            P("dp", None, "tensor"),
            P("dp", "tensor"),
            P(None, None, "tensor", "dp"),
            P("dp"),
            P("tensor", "dp"),
            P("dp"),
            P("dp", None, "tensor"),
            P("tensor", "dp"),
        ),
        check_vma=False,
    )
```

```python
import jax
import jax.numpy as jnp
from jax import lax
from jax.experimental import pallas as pl
from jax.experimental.pallas import tpu as pltpu
from jax.sharding import PartitionSpec as P

BLOCK = 64
NORM_EPS = 1e-06
HEAD_EPS = 1e-05
F32 = jnp.float32
BF16 = jnp.bfloat16
LANES = 128
HALO = 8


def low_dot(left, right, left_dim, right_dim):
    return lax.dot_general(
        left.astype(BF16),
        right.astype(BF16),
        (((left_dim,), (right_dim,)), ((), ())),
        preferred_element_type=F32,
    )


def sigmoid(value):
    return 1.0 / (1.0 + jnp.exp(-value))


def block_masks(rows):
    row = lax.broadcasted_iota(jnp.int32, (rows, rows), 0)
    col = lax.broadcasted_iota(jnp.int32, (rows, rows), 1)
    same = {size: (row // size) == (col // size) for size in (8, 16, 32, 64)}
    strict = jnp.logical_and(same[64], col < row)
    lower = jnp.logical_and(same[64], col <= row)
    eye = (row == col).astype(F32)
    return same, strict, lower, eye


def unit_inverse(system, same, eye):
    base = jnp.where(same[8], system, 0.0)
    square = low_dot(base, base, 1, 0)
    fourth = low_dot(square, square, 1, 0)
    inverse = eye - base
    inverse = inverse + low_dot(inverse, square, 1, 0)
    inverse = inverse + low_dot(inverse, fourth, 1, 0)
    for size in (8, 16, 32):
        off = jnp.where(jnp.logical_and(same[2 * size], jnp.logical_not(same[size])), system, 0.0)
        inverse = inverse - low_dot(inverse, low_dot(off, inverse, 1, 0), 1, 0)
    return inverse


def delayed_rows(previous, current, lag):
    if lag == 0:
        return current
    rows = current.shape[0]
    joined = jnp.concatenate([previous, current], axis=0)
    return joined[HALO - lag : HALO - lag + rows]


def conv_part(proj_ref, before_ref, conv_ref, reach, part, head, head_dim, heads):
    width = heads * head_dim
    column = part * width + head * head_dim
    current = proj_ref[:, column : column + head_dim]
    previous = before_ref[:, column : column + head_dim]
    taps = [conv_ref[part * 4 + lag : part * 4 + lag + 1, head * head_dim : (head + 1) * head_dim] for lag in range(4)]
    shifted = [current]
    for lag in range(1, 4):
        shifted.append(delayed_rows(previous, current, lag) * reach[lag])
    total = taps[0] * shifted[0]
    for lag in range(1, 4):
        total = total + taps[lag] * shifted[lag]
    return total, shifted, taps


def stack_heads(pieces, index):
    return jnp.concatenate([piece[index * BLOCK : (index + 1) * BLOCK] for piece in pieces], axis=0)


def forward_kernel(
    proj_ref, before_ref, logit_ref, pos_ref, valid_ref, conv_ref, gain_ref,
    mixed_ref, recall_ref, start_ref, inverse_ref, update_ref, weight_ref,
    state_ref, *, heads, head_dim,
):
    rows = proj_ref.shape[0]
    blocks = rows // BLOCK
    stacked = heads * BLOCK

    @pl.when(pl.program_id(0) == 0)
    def _():
        state_ref[...] = jnp.zeros_like(state_ref)

    pos = pos_ref[...]
    valid = valid_ref[...]
    reach = [None] + [(pos >= lag).astype(F32) for lag in range(1, 4)]
    parts = [[], [], []]
    strengths = []
    for head in range(heads):
        for part in range(3):
            total, _, _ = conv_part(proj_ref, before_ref, conv_ref, reach, part, head, head_dim, heads)
            value = total * sigmoid(total)
            if part < 2:
                scale = lax.rsqrt(jnp.sum(value * value, -1, keepdims=True) + NORM_EPS)
                if part == 0:
                    scale = scale * head_dim ** (-0.5)
                value = value * scale
            parts[part].append(value)
        strengths.append(sigmoid(logit_ref[:, head : head + 1]) * valid)
    same, strict, lower, eye = block_masks(stacked)
    local = []
    for index in range(blocks):
        queries = stack_heads(parts[0], index).astype(BF16)
        keys = stack_heads(parts[1], index)
        values = stack_heads(parts[2], index)
        strength = stack_heads(strengths, index)
        keys_low = keys.astype(BF16)
        gram = low_dot(keys_low, keys_low, 1, 1)
        system = jnp.where(strict, strength * gram, 0.0)
        inverse = unit_inverse(system, same, eye).astype(BF16)
        weighted = low_dot(inverse, strength * keys, 1, 0).astype(BF16)
        fresh = low_dot(inverse, strength * values, 1, 0)
        scores = jnp.where(lower, low_dot(queries, keys_low, 1, 1), 0.0).astype(BF16)
        inverse_ref[index] = inverse
        weight_ref[index] = weighted
        local.append((queries, keys_low, weighted, fresh, scores))
    for index in range(blocks):
        queries, keys_low, weighted, fresh, scores = local[index]
        keep = (pos[index * BLOCK : index * BLOCK + 1] != 0).astype(F32)
        updates = []
        carried = []
        for head in range(heads):
            span = slice(head * BLOCK, (head + 1) * BLOCK)
            state = state_ref[head] * keep
            state_low = state.astype(BF16)
            start_ref[index, head] = state_low
            update = fresh[span] - low_dot(weighted[span], state_low, 1, 1)
            update_low = update.astype(BF16)
            updates.append(update_low)
            carried.append(low_dot(queries[span], state_low, 1, 1))
            state_ref[head] = state + low_dot(update_low, keys_low[span], 0, 0)
        update_all = jnp.concatenate(updates, axis=0)
        update_ref[index] = update_all
        recall_all = jnp.concatenate(carried, axis=0) + low_dot(scores, update_all, 1, 0)
        scale = lax.rsqrt(jnp.mean(recall_all * recall_all, -1, keepdims=True) + HEAD_EPS)
        normed = recall_all * scale * gain_ref[...]
        here = slice(index * BLOCK, (index + 1) * BLOCK)
        for head in range(heads):
            span = slice(head * BLOCK, (head + 1) * BLOCK)
            column = slice(head * head_dim, (head + 1) * head_dim)
            recall_ref[here, column] = recall_all[span]
            mixed_ref[here, column] = (normed[span] * valid[here]).astype(BF16)


def backward_kernel(
    proj_ref, before_ref, logit_ref, pos_ref, after_ref, valid_ref, conv_ref, gain_ref,
    recall_ref, start_ref, inverse_ref, update_ref, weight_ref, mixed_grad_ref,
    proj_grad_ref, conv_grad_ref, gain_grad_ref,
    state_ref, halo_ref, *, heads, head_dim,
):
    rows = proj_ref.shape[0]
    blocks = rows // BLOCK
    stacked = heads * BLOCK
    width = heads * head_dim

    @pl.when(pl.program_id(0) == 0)
    def _():
        state_ref[...] = jnp.zeros_like(state_ref)
        halo_ref[...] = jnp.zeros_like(halo_ref)
        conv_grad_ref[...] = jnp.zeros_like(conv_grad_ref)
        gain_grad_ref[...] = jnp.zeros_like(gain_grad_ref)

    pos = pos_ref[...]
    valid = valid_ref[...]
    reach = [None] + [(pos >= lag).astype(F32) for lag in range(1, 4)]
    pos_ahead = jnp.concatenate([pos, after_ref[...]], axis=0)
    reach_ahead = [None] + [(pos_ahead >= lag).astype(F32) for lag in range(1, 4)]
    gain = gain_ref[...]
    parts = [[], [], []]
    gates = []
    recall_grads = []
    gain_grad = jnp.zeros((1, head_dim), F32)
    for head in range(heads):
        for part in range(3):
            total, _, _ = conv_part(proj_ref, before_ref, conv_ref, reach, part, head, head_dim, heads)
            value = total * sigmoid(total)
            if part < 2:
                scale = lax.rsqrt(jnp.sum(value * value, -1, keepdims=True) + NORM_EPS)
                if part == 0:
                    scale = scale * head_dim ** (-0.5)
                value = value * scale
            parts[part].append(value)
        gates.append(sigmoid(logit_ref[:, head : head + 1]))
        column = slice(head * head_dim, (head + 1) * head_dim)
        recall = recall_ref[:, column]
        pulled = mixed_grad_ref[:, column] * valid
        scale = lax.rsqrt(jnp.mean(recall * recall, -1, keepdims=True) + HEAD_EPS)
        normed = recall * scale
        gain_grad = gain_grad + jnp.sum(pulled * normed, 0, keepdims=True)
        pulled = pulled * gain
        recall_grads.append(
            scale * (pulled - normed * jnp.mean(normed * pulled, -1, keepdims=True))
        )
    gain_grad_ref[...] += gain_grad
    strengths = [gate * valid for gate in gates]
    same, strict, lower, eye = block_masks(stacked)
    query_grads = [None] * blocks
    key_grads = [None] * blocks
    value_grads = [None] * blocks
    strength_grads = [None] * blocks
    for index in range(blocks - 1, -1, -1):
        queries = stack_heads(parts[0], index).astype(BF16)
        keys = stack_heads(parts[1], index).astype(BF16)
        values = stack_heads(parts[2], index)
        strength = stack_heads(strengths, index)
        out_grad = stack_heads(recall_grads, index).astype(BF16)
        inverse = inverse_ref[index]
        weighted = weight_ref[index]
        update = update_ref[index]
        gram = low_dot(keys, keys, 1, 1)
        scores = jnp.where(lower, low_dot(queries, keys, 1, 1), 0.0).astype(BF16)
        local_grad = low_dot(scores, out_grad, 0, 0)
        score_grad = jnp.where(lower, low_dot(out_grad, update, 1, 1), 0.0).astype(BF16)
        keep = (pos[index * BLOCK : index * BLOCK + 1] != 0).astype(F32)
        update_grads = []
        query_carried = []
        key_carried = []
        misses = []
        starts = []
        for head in range(heads):
            span = slice(head * BLOCK, (head + 1) * BLOCK)
            ahead = state_ref[head]
            ahead_low = ahead.astype(BF16)
            start = start_ref[index, head]
            starts.append(start)
            update_grad = local_grad[span] + low_dot(keys[span], ahead_low, 1, 1)
            update_grad_low = update_grad.astype(BF16)
            update_grads.append(update_grad_low)
            carried = ahead + low_dot(out_grad[span], queries[span], 0, 0)
            carried = carried - low_dot(update_grad_low, weighted[span], 0, 0)
            state_ref[head] = carried * keep
            query_carried.append(low_dot(out_grad[span], start, 1, 0))
            key_carried.append(low_dot(update[span], ahead_low, 1, 0))
            misses.append(values[span] - low_dot(keys[span], start, 1, 1))
        miss_grad = low_dot(inverse, jnp.concatenate(update_grads, axis=0), 0, 0)
        miss = jnp.concatenate(misses, axis=0)
        system_grad = jnp.where(strict, -low_dot(miss_grad, update, 1, 1), 0.0)
        strength_grads[index] = jnp.sum(miss_grad * miss, -1, keepdims=True) + jnp.sum(
            system_grad * gram, -1, keepdims=True
        )
        gram_grad = (strength * system_grad).astype(BF16)
        value_grad = strength * miss_grad
        value_low = value_grad.astype(BF16)
        value_grads[index] = value_grad
        query_grads[index] = jnp.concatenate(query_carried, axis=0) + low_dot(score_grad, keys, 1, 0)
        key_grad = jnp.concatenate(key_carried, axis=0) + low_dot(score_grad, queries, 0, 0)
        key_grad = key_grad + low_dot(gram_grad, keys, 1, 0) + low_dot(gram_grad, keys, 0, 0)
        key_state = [
            low_dot(value_low[head * BLOCK : (head + 1) * BLOCK], starts[head], 1, 0)
            for head in range(heads)
        ]
        key_grads[index] = key_grad - jnp.concatenate(key_state, axis=0)
    grads = [query_grads, key_grads, value_grads]
    logit_grads = []
    for head in range(heads):
        span = slice(head * BLOCK, (head + 1) * BLOCK)
        gate = gates[head]
        pulled = jnp.concatenate([strength_grads[index][span] for index in range(blocks)], axis=0)
        logit_grads.append(pulled * valid * gate * (1.0 - gate))
        for part in range(3):
            pulled = jnp.concatenate([grads[part][index][span] for index in range(blocks)], axis=0)
            total, shifted, taps = conv_part(
                proj_ref, before_ref, conv_ref, reach, part, head, head_dim, heads
            )
            gate_part = sigmoid(total)
            value = total * gate_part
            if part < 2:
                scale = lax.rsqrt(jnp.sum(value * value, -1, keepdims=True) + NORM_EPS)
                normed = value * scale
                pulled = scale * (pulled - normed * jnp.sum(normed * pulled, -1, keepdims=True))
                if part == 0:
                    pulled = pulled * head_dim ** (-0.5)
            pre_grad = pulled * gate_part * (1.0 + total * (1.0 - gate_part))
            column = slice(part * width + head * head_dim, part * width + (head + 1) * head_dim)
            tap_column = slice(head * head_dim, (head + 1) * head_dim)
            for lag in range(4):
                conv_grad_ref[part * 4 + lag : part * 4 + lag + 1, tap_column] += jnp.sum(
                    pre_grad * shifted[lag], 0, keepdims=True
                )
            joined = jnp.concatenate([pre_grad, halo_ref[:, column]], axis=0)
            total_grad = taps[0] * pre_grad
            for lag in range(1, 4):
                total_grad = total_grad + taps[lag] * (joined * reach_ahead[lag])[lag : lag + rows]
            proj_grad_ref[:, column] = total_grad.astype(BF16)
            halo_ref[:, column] = pre_grad[:HALO]
    blank = jnp.zeros((rows, LANES - heads), F32)
    proj_grad_ref[:, 3 * width :] = jnp.concatenate(logit_grads + [blank], axis=1).astype(BF16)


def mixer_specs(rows, columns, order):
    blocks = rows // BLOCK
    ratio = rows // HALO

    def whole(*shape):
        return pl.BlockSpec(shape, lambda step: (0,) * len(shape))

    def by_rows(size, column=0):
        return pl.BlockSpec((rows, size), lambda step: (order(step), column))

    def by_blocks(*tail):
        return pl.BlockSpec((blocks,) + tail, lambda step: (order(step),) + (0,) * len(tail))

    before = pl.BlockSpec(
        (HALO, columns), lambda step: (jnp.maximum(order(step) * ratio - 1, 0), 0)
    )
    return whole, by_rows, by_blocks, before


def mixer_forward(projected, conv_rows, head_gain, pos, valid, heads):
    slots = projected.shape[0]
    head_dim = head_gain.shape[1]
    width = heads * head_dim
    columns = 3 * width
    rows = slots // lax.axis_size("tensor")
    steps = slots // rows
    stacked = heads * BLOCK
    block_count = slots // BLOCK
    whole, by_rows, by_blocks, before = mixer_specs(rows, columns, lambda step: step)
    return pl.pallas_call(
        lambda *refs: forward_kernel(*refs, heads=heads, head_dim=head_dim),
        grid=(steps,),
        in_specs=[
            by_rows(columns),
            before,
            by_rows(LANES, columns // LANES),
            by_rows(1),
            by_rows(1),
            whole(12, width),
            whole(1, head_dim),
        ],
        out_specs=[
            by_rows(width),
            by_rows(width),
            by_blocks(heads, head_dim, head_dim),
            by_blocks(stacked, stacked),
            by_blocks(stacked, head_dim),
            by_blocks(stacked, head_dim),
        ],
        scratch_shapes=[pltpu.VMEM((heads, head_dim, head_dim), F32)],
        out_shape=[
            jax.ShapeDtypeStruct((slots, width), BF16),
            jax.ShapeDtypeStruct((slots, width), F32),
            jax.ShapeDtypeStruct((block_count, heads, head_dim, head_dim), BF16),
            jax.ShapeDtypeStruct((block_count, stacked, stacked), BF16),
            jax.ShapeDtypeStruct((block_count, stacked, head_dim), BF16),
            jax.ShapeDtypeStruct((block_count, stacked, head_dim), BF16),
        ],
        name="mixer_forward",
    )(projected, projected, projected, pos, valid, conv_rows, head_gain)


def mixer_backward(projected, conv_rows, head_gain, pos, valid, heads, kept, mixed_grad):
    slots = projected.shape[0]
    head_dim = head_gain.shape[1]
    width = heads * head_dim
    columns = 3 * width
    rows = slots // lax.axis_size("tensor")
    steps = slots // rows
    stacked = heads * BLOCK
    ratio = rows // HALO
    recall, start, inverse, update, weighted = kept
    pos_padded = jnp.pad(pos, ((0, HALO), (0, 0)))
    whole, by_rows, by_blocks, before = mixer_specs(rows, columns, lambda step: steps - 1 - step)
    return pl.pallas_call(
        lambda *refs: backward_kernel(*refs, heads=heads, head_dim=head_dim),
        grid=(steps,),
        in_specs=[
            by_rows(columns),
            before,
            by_rows(LANES, columns // LANES),
            by_rows(1),
            pl.BlockSpec((HALO, 1), lambda step: ((steps - step) * ratio, 0)),
            by_rows(1),
            whole(12, width),
            whole(1, head_dim),
            by_rows(width),
            by_blocks(heads, head_dim, head_dim),
            by_blocks(stacked, stacked),
            by_blocks(stacked, head_dim),
            by_blocks(stacked, head_dim),
            by_rows(width),
        ],
        out_specs=[by_rows(columns + LANES), whole(12, width), whole(1, head_dim)],
        scratch_shapes=[
            pltpu.VMEM((heads, head_dim, head_dim), F32),
            pltpu.VMEM((HALO, columns), F32),
        ],
        out_shape=[
            jax.ShapeDtypeStruct((slots, columns + LANES), BF16),
            jax.ShapeDtypeStruct((12, width), F32),
            jax.ShapeDtypeStruct((1, head_dim), F32),
        ],
        name="mixer_backward",
    )(
        projected, projected, projected, pos, pos_padded, valid, conv_rows, head_gain,
        recall, start, inverse, update, weighted, mixed_grad,
    )


def doc_layout(length_pair, slot_count):
    first_end = (length_pair[0] + BLOCK - 1) // BLOCK * BLOCK
    second_end = first_end + (length_pair[1] + BLOCK - 1) // BLOCK * BLOCK
    places = jnp.arange(slot_count, dtype=jnp.int32)
    in_first = places < first_end
    in_second = jnp.logical_and(places >= first_end, places < second_end)
    doc_begin = jnp.where(in_first, 0, jnp.where(in_second, first_end, second_end))
    doc_limit = jnp.where(in_first, length_pair[0], jnp.where(in_second, length_pair[1], 0))
    offset = places - doc_begin
    is_valid = (offset < doc_limit).astype(F32)
    return offset.astype(F32)[:, None], is_valid[:, None]


def ring_shift(value, step):
    size = lax.axis_size("tensor")
    return lax.ppermute(value, "tensor", [(place, (place + step) % size) for place in range(size)])


def held(value, *others):
    return lax.optimization_barrier((value, others))[0]


def piece_start(step, count):
    size = lax.axis_size("tensor")
    return lax.rem(lax.axis_index("tensor") + step, size) * count


def gather_rows(rows, *token, mid=()):
    size = lax.axis_size("tensor")
    count = rows.shape[0]
    half = count // 2
    rows = held(rows, token)
    full = jnp.zeros((size * count, rows.shape[1]), rows.dtype)

    def put(full, piece, step, at=0):
        return lax.dynamic_update_slice(full, piece, (piece_start(step, count) + at, 0))

    full = put(full, rows, 0)
    from_left = rows
    from_right = rows
    for step in range(1, size // 2):
        from_left = ring_shift(from_left, 1)
        from_right = ring_shift(from_right, -1)
        full = put(full, from_left, size - step)
        full = put(full, from_right, step)
    from_left_half, from_right_half = from_left[:half], from_right[half:]
    if mid:
        from_left_half, from_right_half = held((from_left_half, from_right_half), mid)
    far = ring_shift(from_left_half, 1), ring_shift(from_right_half, -1)
    full = put(full, far[0], size // 2)
    full = put(full, far[1], size // 2, half)
    return full, (from_left, from_right), far


def ring_rows(low, step, at, length):
    count = low.shape[0] // lax.axis_size("tensor")
    start = piece_start(step, count) + at
    return lax.dynamic_slice(low, (start, 0), (length, low.shape[1])).astype(F32)


def scatter_rows_begin(partial, *token):
    size = lax.axis_size("tensor")
    half = partial.shape[0] // size // 2
    low = held(partial, token)
    to_right = ring_shift(ring_rows(low, size // 2, 0, half).astype(BF16), 1)
    to_left = ring_shift(ring_rows(low, size // 2, half, half).astype(BF16), -1)
    return low, (to_right, to_left)


def scatter_rows_end(state, *token):
    size = lax.axis_size("tensor")
    low, (to_right, to_left) = state
    count = low.shape[0] // size
    half = count // 2
    if token:
        to_right, to_left = held((to_right, to_left), token)
    for step in range(size // 2 - 1, 0, -1):
        right = ring_rows(low, step, 0, count)
        left = ring_rows(low, size - step, 0, count)
        if step == size // 2 - 1:
            right = joined([right[:half] + to_right.astype(F32), right[half:]])
            left = joined([left[:half], left[half:] + to_left.astype(F32)])
        else:
            right = right + to_right.astype(F32)
            left = left + to_left.astype(F32)
        to_right = ring_shift(right.astype(BF16), 1)
        to_left = ring_shift(left.astype(BF16), -1)
    total = ring_rows(low, 0, 0, count) + to_right.astype(F32) + to_left.astype(F32)
    return total, (to_right, to_left)


def scatter_rows(partial, *token, mid=()):
    state = scatter_rows_begin(partial, *token)
    total, last = scatter_rows_end(state, *mid)
    return total, state[1], last


def dot(left, right, left_dim, right_dim, out_type=F32):
    return lax.dot_general(
        left, right, (((left_dim,), (right_dim,)), ((), ())), preferred_element_type=out_type
    )


def gather_dp(value):
    return lax.all_gather(value, "dp", axis=0, tiled=True)


def scatter_dp(value):
    return lax.psum_scatter(value, "dp", scatter_dimension=0, tiled=True)


def row_scale(values):
    return lax.rsqrt(jnp.mean(values * values, -1, keepdims=True) + NORM_EPS)


def norm_pull(values, pulled):
    scale = row_scale(values)
    normed = values * scale
    return scale * (pulled - normed * jnp.mean(normed * pulled, -1, keepdims=True))


def joined(parts):
    return jnp.concatenate(parts, axis=0)


def per_device(
    tokens, cotangent, doc_lengths, attn_gain, w_qkv, w_beta, conv_weight, head_gain,
    w_out, ffn_gain, w_gate_up, w_down,
):
    batches, local_rows, width = tokens.shape
    size = lax.axis_size("tensor")
    dp_size = lax.axis_size("dp")
    slots = local_rows * size
    shard = w_qkv.shape[0]
    heads = w_beta.shape[1]
    units = w_down.shape[0]
    head_share = head_gain.shape[0]
    head_dim = head_share * dp_size
    columns = 3 * heads * head_dim
    conv_share = 12 * heads * head_share
    small_share = conv_share + head_share
    extra = -(-small_share // shard)
    small_at = columns + heads

    attn_column = attn_gain.astype(F32)[:, None]
    ffn_column = ffn_gain.astype(F32)[:, None]
    qkv_rows = jnp.concatenate([w_qkv.reshape(shard, columns), w_beta], axis=1).astype(F32)
    small = jnp.concatenate(
        [conv_weight.reshape(-1), head_gain, jnp.zeros((extra * shard - small_share,), BF16)]
    ).reshape(shard, extra)
    blank = jnp.zeros((shard, LANES - heads - extra), BF16)
    full_proj = gather_dp(
        jnp.concatenate([(attn_column * qkv_rows).astype(BF16), small, blank], axis=1)
    )
    full_out = gather_dp(w_out.T)
    gate_up_rows = w_gate_up.reshape(shard, 2 * units).astype(F32)
    full_gate_up = gather_dp((ffn_column * gate_up_rows).astype(BF16))
    full_down = gather_dp(w_down.T)
    small = full_proj[:, small_at : small_at + extra].astype(F32).reshape(dp_size, extra * shard)
    full_conv = small[:, :conv_share].reshape(dp_size, 12, heads, head_share)
    full_conv = jnp.transpose(full_conv, (1, 2, 0, 3)).reshape(12, heads * head_dim)
    full_head_gain = small[:, conv_share:small_share].reshape(1, head_dim)

    rows = [tokens[index].astype(F32) for index in range(batches)]
    layouts = [doc_layout(doc_lengths[index, 0], slots) for index in range(batches)]

    def mix(index, projected, *beside):
        mixed, *kept = mixer_forward(
            projected, full_conv, full_head_gain, *layouts[index], heads
        )
        return mixed, kept, dot(held(mixed, beside), full_out, 1, 1, BF16)

    def after_mixer(index, branch):
        hidden = rows[index] + branch
        return hidden, (hidden * row_scale(hidden)).astype(BF16)

    def feed(ffn_full):
        gate_up = dot(ffn_full, full_gate_up, 1, 0)
        gate = gate_up[:, :units]
        activated = (gate * sigmoid(gate) * gate_up[:, units:]).astype(BF16)
        return gate_up, activated

    def feed_back(gate_up, cot_full, *beside):
        grad_act = dot(cot_full, full_down, 1, 0)
        gate = gate_up[:, :units]
        up = gate_up[:, units:]
        opened = sigmoid(gate)
        grad_gate = grad_act * up * opened * (1.0 + gate * (1.0 - opened))
        grad_up = grad_act * (gate * opened)
        grad_gate_up = jnp.concatenate([grad_gate, grad_up], axis=1).astype(BF16)
        return grad_gate_up, dot(held(grad_gate_up, beside), full_gate_up, 1, 1, BF16)

    def before_ffn(index, hidden, pulled):
        return cotangent[index].astype(F32) + norm_pull(hidden, pulled)

    attn_in = [(rows[index] * row_scale(rows[index])).astype(BF16) for index in range(batches)]
    attn_0, first, last = gather_rows(attn_in[0])
    attn_1, attn_first, _ = gather_rows(attn_in[1], last, full_proj)
    cot_0, cot_first, _ = gather_rows(cotangent[0], last, full_proj)
    proj_0 = dot(attn_0, full_proj, 1, 0)
    mixed_0, kept_0, part_0 = mix(0, proj_0, attn_first, cot_first)

    branch, first, last = scatter_rows(part_0)
    proj_1 = dot(attn_1, full_proj, 1, 0)
    mixed_1, kept_1, part_1 = mix(1, held(proj_1, first), last, cot_0)
    hidden_0, ffn_in = after_mixer(0, branch)
    cot_1 = lax.all_gather(held(cotangent[1], full_down, part_1), "tensor", axis=0, tiled=True)

    ffn_0, ffn_first, _ = gather_rows(ffn_in, part_1, full_gate_up)
    branch, first, last = scatter_rows(part_1, ffn_first)
    gate_up_0, act_0 = feed(held(ffn_0, first))
    grad_gate_up_0, part_0 = feed_back(gate_up_0, cot_0, last)
    hidden_1, ffn_in = after_mixer(1, branch)

    ffn_1, ffn_first, _ = gather_rows(ffn_in)
    down_0 = dot(held(act_0, part_0), full_down, 1, 1, BF16)
    down_grad = dot(held(cot_0, down_0), act_0, 0, 0, BF16)
    pulled, first, last = scatter_rows(part_0, ffn_first)
    gate_up_grad = dot(held(ffn_0, down_grad, ffn_first), grad_gate_up_0, 0, 0, BF16)
    gate_up_1, act_1 = feed(held(ffn_1, first, gate_up_grad))
    down_state = scatter_rows_begin(down_0, first)
    grad_gate_up_1, part_1 = feed_back(gate_up_1, cot_1, last, down_state[1])
    grad_hidden_0 = before_ffn(0, hidden_0, pulled)

    branch_0, first, last = gather_rows(grad_hidden_0.astype(BF16))
    down_grad = (down_grad + dot(held(cot_1, part_1, first), act_1, 0, 0)).astype(BF16)
    pulled, first, last = scatter_rows(part_1, first)
    gate_up_grad = gate_up_grad + dot(held(ffn_1, first, branch_0, down_grad), grad_gate_up_1, 0, 0)
    gate_up_grad = gate_up_grad.astype(BF16)
    grad_hidden_1 = before_ffn(1, hidden_1, pulled)

    branch_in = held(grad_hidden_1.astype(BF16), gate_up_grad)
    branch_1, branch_first, _ = gather_rows(branch_in)
    down_grad = scatter_dp(down_grad)
    gate_up_grad = scatter_dp(gate_up_grad)
    down_1 = dot(held(act_1, branch_in), full_down, 1, 1, BF16)
    grad_mixed = dot(held(branch_0, branch_in), full_out, 1, 0)
    grad_mixed = held(grad_mixed, branch_first, down_1)
    grad_proj_0, conv_grad_0, gain_grad_0 = mixer_backward(
        proj_0, full_conv, full_head_gain, *layouts[0], heads, kept_0, grad_mixed
    )
    lower_0, down_last = scatter_rows_end(down_state, branch_first)
    part_0 = dot(held(grad_proj_0, branch_1, down_last), full_proj, 1, 1, BF16)

    pulled, first, last = scatter_rows(part_0)
    out_grad = dot(
        joined([held(branch_0, part_0), branch_1]), joined([mixed_0, mixed_1]), 0, 0, BF16
    )
    grad_mixed = dot(held(branch_1, part_0), full_out, 1, 0)
    input_rows_0 = grad_hidden_0 + norm_pull(rows[0], pulled)
    grad_mixed = held(grad_mixed, first, out_grad)
    out_grad = scatter_dp(out_grad)
    grad_proj_1, conv_grad_1, gain_grad_1 = mixer_backward(
        proj_1, full_conv, full_head_gain, *layouts[1], heads, kept_1, grad_mixed
    )
    part_1 = dot(held(grad_proj_1, last), full_proj, 1, 1, BF16)
    attn_all = joined([held(attn_0, last), attn_1])
    pulled, first, last = scatter_rows(part_1, last, down_grad, gate_up_grad)
    down_out = down_grad.T.astype(F32)
    proj_grad = dot(attn_all, joined([grad_proj_0, grad_proj_1]), 0, 0, BF16)
    conv_grad = (conv_grad_0 + conv_grad_1).reshape(12, heads, dp_size, head_share)
    conv_grad = jnp.transpose(conv_grad, (2, 0, 1, 3)).reshape(dp_size, conv_share)
    head_gain_grad = (gain_grad_0 + gain_grad_1).reshape(dp_size, head_share)
    small_grad = jnp.concatenate(
        [conv_grad, head_gain_grad, jnp.zeros((dp_size, extra * shard - small_share), F32)], axis=1
    )
    small_grad = small_grad.reshape(dp_size * shard, extra).astype(BF16)
    small_grad = jnp.pad(small_grad, ((0, 0), (small_at, LANES - heads - extra)))
    proj_grad = scatter_dp(proj_grad + small_grad)
    gate_up_grad = gate_up_grad.astype(F32)
    gate_up_out = (gate_up_grad * ffn_column).reshape(shard, 2, units)
    ffn_gain_grad = jnp.sum(gate_up_grad * gate_up_rows, axis=1)
    out_out = out_grad.T.astype(F32)
    lower_1, first, last = scatter_rows(
        down_1, last, down_out, mid=(gate_up_out, ffn_gain_grad, out_out)
    )
    proj_grad = held(proj_grad, first)
    input_rows_1 = grad_hidden_1 + norm_pull(rows[1], pulled)
    layer_rows_0 = (hidden_0 + lower_0).astype(BF16)
    layer_rows_1 = (hidden_1 + lower_1).astype(BF16)

    proj_grad = proj_grad.astype(F32)
    small_grad = proj_grad[:, small_at : small_at + extra].reshape(extra * shard)
    gain_grads = jnp.concatenate(
        [
            jnp.sum(proj_grad[:, :small_at] * qkv_rows, axis=1),
            ffn_gain_grad,
            small_grad[conv_share:small_share],
        ]
    )[None]
    gain_grads = held(gain_grads, last)
    total = gain_grads
    for step in range(1, size):
        total = total + ring_shift(gain_grads, step)
    total = total[0]
    proj_grad = proj_grad[:, :small_at] * attn_column
    return (
        jnp.stack([layer_rows_0, layer_rows_1]),
        jnp.stack([input_rows_0, input_rows_1]),
        total[:shard],
        proj_grad[:, :columns].reshape(shard, 3, -1),
        proj_grad[:, columns:],
        small_grad[:conv_share].reshape(3, 4, heads, head_share),
        total[2 * shard :],
        out_out,
        total[shard : 2 * shard],
        gate_up_out,
        down_out,
    )


def solution(mesh):
    return jax.shard_map(
        per_device,
        mesh=mesh,
        in_specs=(
            P(None, ("dp", "tensor"), None),
            P(None, ("dp", "tensor"), None),
            P(None, "dp", None),
            P("dp"),
            P("dp", None, "tensor"),
            P("dp", "tensor"),
            P(None, None, "tensor", "dp"),
            P("dp"),
            P("tensor", "dp"),
            P("dp"),
            P("dp", None, "tensor"),
            P("tensor", "dp"),
        ),
        out_specs=(
            P(None, ("dp", "tensor"), None),
            P(None, ("dp", "tensor"), None),
            P("dp"),
            P("dp", None, "tensor"),
            P("dp", "tensor"),
            P(None, None, "tensor", "dp"),
            P("dp"),
            P("tensor", "dp"),
            P("dp"),
            P("dp", None, "tensor"),
            P("tensor", "dp"),
        ),
        check_vma=False,
    )
```

```python
import jax
import jax.numpy as jnp
from jax import lax
from jax.experimental import pallas as pl
from jax.experimental.pallas import tpu as pltpu
from jax.sharding import PartitionSpec as P

BLOCK = 64
NORM_EPS = 1e-06
HEAD_EPS = 1e-05
F32 = jnp.float32
BF16 = jnp.bfloat16
LANES = 128
HALO = 8


def low_dot(left, right, left_dim, right_dim):
    return lax.dot_general(
        left.astype(BF16),
        right.astype(BF16),
        (((left_dim,), (right_dim,)), ((), ())),
        preferred_element_type=F32,
    )


def sigmoid(value):
    return 1.0 / (1.0 + jnp.exp(-value))


def block_masks(rows):
    row = lax.broadcasted_iota(jnp.int32, (rows, rows), 0)
    col = lax.broadcasted_iota(jnp.int32, (rows, rows), 1)
    same = {size: (row // size) == (col // size) for size in (8, 16, 32, 64)}
    strict = jnp.logical_and(same[64], col < row)
    lower = jnp.logical_and(same[64], col <= row)
    eye = (row == col).astype(F32)
    return same, strict, lower, eye


def unit_inverse(system, same, eye):
    base = jnp.where(same[8], system, 0.0)
    square = low_dot(base, base, 1, 0)
    fourth = low_dot(square, square, 1, 0)
    inverse = eye - base
    inverse = inverse + low_dot(inverse, square, 1, 0)
    inverse = inverse + low_dot(inverse, fourth, 1, 0)
    for size in (8, 16, 32):
        off = jnp.where(jnp.logical_and(same[2 * size], jnp.logical_not(same[size])), system, 0.0)
        inverse = inverse - low_dot(inverse, low_dot(off, inverse, 1, 0), 1, 0)
    return inverse


def delayed_rows(previous, current, lag):
    if lag == 0:
        return current
    rows = current.shape[0]
    joined = jnp.concatenate([previous, current], axis=0)
    return joined[HALO - lag : HALO - lag + rows]


def conv_part(proj_ref, before_ref, conv_ref, reach, part, head, head_dim, heads):
    width = heads * head_dim
    column = part * width + head * head_dim
    current = proj_ref[:, column : column + head_dim]
    previous = before_ref[:, column : column + head_dim]
    taps = [conv_ref[part * 4 + lag : part * 4 + lag + 1, head * head_dim : (head + 1) * head_dim] for lag in range(4)]
    shifted = [current]
    for lag in range(1, 4):
        shifted.append(delayed_rows(previous, current, lag) * reach[lag])
    total = taps[0] * shifted[0]
    for lag in range(1, 4):
        total = total + taps[lag] * shifted[lag]
    return total, shifted, taps


def stack_heads(pieces, index):
    return jnp.concatenate([piece[index * BLOCK : (index + 1) * BLOCK] for piece in pieces], axis=0)


def forward_kernel(
    proj_ref, before_ref, logit_ref, pos_ref, valid_ref, conv_ref, gain_ref,
    mixed_ref, recall_ref, start_ref, inverse_ref, update_ref, weight_ref,
    state_ref, *, heads, head_dim,
):
    rows = proj_ref.shape[0]
    blocks = rows // BLOCK
    stacked = heads * BLOCK

    @pl.when(pl.program_id(0) == 0)
    def _():
        state_ref[...] = jnp.zeros_like(state_ref)

    pos = pos_ref[...]
    valid = valid_ref[...]
    reach = [None] + [(pos >= lag).astype(F32) for lag in range(1, 4)]
    parts = [[], [], []]
    strengths = []
    for head in range(heads):
        for part in range(3):
            total, _, _ = conv_part(proj_ref, before_ref, conv_ref, reach, part, head, head_dim, heads)
            value = total * sigmoid(total)
            if part < 2:
                scale = lax.rsqrt(jnp.sum(value * value, -1, keepdims=True) + NORM_EPS)
                if part == 0:
                    scale = scale * head_dim ** (-0.5)
                value = value * scale
            parts[part].append(value)
        strengths.append(sigmoid(logit_ref[:, head : head + 1]) * valid)
    same, strict, lower, eye = block_masks(stacked)
    local = []
    for index in range(blocks):
        queries = stack_heads(parts[0], index).astype(BF16)
        keys = stack_heads(parts[1], index)
        values = stack_heads(parts[2], index)
        strength = stack_heads(strengths, index)
        keys_low = keys.astype(BF16)
        gram = low_dot(keys_low, keys_low, 1, 1)
        system = jnp.where(strict, strength * gram, 0.0)
        inverse = unit_inverse(system, same, eye).astype(BF16)
        weighted = low_dot(inverse, strength * keys, 1, 0).astype(BF16)
        fresh = low_dot(inverse, strength * values, 1, 0)
        scores = jnp.where(lower, low_dot(queries, keys_low, 1, 1), 0.0).astype(BF16)
        inverse_ref[index] = inverse
        weight_ref[index] = weighted
        local.append((queries, keys_low, weighted, fresh, scores))
    for index in range(blocks):
        queries, keys_low, weighted, fresh, scores = local[index]
        keep = (pos[index * BLOCK : index * BLOCK + 1] != 0).astype(F32)
        updates = []
        carried = []
        for head in range(heads):
            span = slice(head * BLOCK, (head + 1) * BLOCK)
            state = state_ref[head] * keep
            state_low = state.astype(BF16)
            start_ref[index, head] = state_low
            update = fresh[span] - low_dot(weighted[span], state_low, 1, 1)
            update_low = update.astype(BF16)
            updates.append(update_low)
            carried.append(low_dot(queries[span], state_low, 1, 1))
            state_ref[head] = state + low_dot(update_low, keys_low[span], 0, 0)
        update_all = jnp.concatenate(updates, axis=0)
        update_ref[index] = update_all
        recall_all = jnp.concatenate(carried, axis=0) + low_dot(scores, update_all, 1, 0)
        scale = lax.rsqrt(jnp.mean(recall_all * recall_all, -1, keepdims=True) + HEAD_EPS)
        normed = recall_all * scale * gain_ref[...]
        here = slice(index * BLOCK, (index + 1) * BLOCK)
        for head in range(heads):
            span = slice(head * BLOCK, (head + 1) * BLOCK)
            column = slice(head * head_dim, (head + 1) * head_dim)
            recall_ref[here, column] = recall_all[span]
            mixed_ref[here, column] = (normed[span] * valid[here]).astype(BF16)


def backward_kernel(
    proj_ref, before_ref, logit_ref, pos_ref, after_ref, valid_ref, conv_ref, gain_ref,
    recall_ref, start_ref, inverse_ref, update_ref, weight_ref, mixed_grad_ref,
    proj_grad_ref, conv_grad_ref, gain_grad_ref,
    state_ref, halo_ref, *, heads, head_dim,
):
    rows = proj_ref.shape[0]
    blocks = rows // BLOCK
    stacked = heads * BLOCK
    width = heads * head_dim

    @pl.when(pl.program_id(0) == 0)
    def _():
        state_ref[...] = jnp.zeros_like(state_ref)
        halo_ref[...] = jnp.zeros_like(halo_ref)
        conv_grad_ref[...] = jnp.zeros_like(conv_grad_ref)
        gain_grad_ref[...] = jnp.zeros_like(gain_grad_ref)

    pos = pos_ref[...]
    valid = valid_ref[...]
    reach = [None] + [(pos >= lag).astype(F32) for lag in range(1, 4)]
    pos_ahead = jnp.concatenate([pos, after_ref[...]], axis=0)
    reach_ahead = [None] + [(pos_ahead >= lag).astype(F32) for lag in range(1, 4)]
    gain = gain_ref[...]
    parts = [[], [], []]
    gates = []
    recall_grads = []
    gain_grad = jnp.zeros((1, head_dim), F32)
    for head in range(heads):
        for part in range(3):
            total, _, _ = conv_part(proj_ref, before_ref, conv_ref, reach, part, head, head_dim, heads)
            value = total * sigmoid(total)
            if part < 2:
                scale = lax.rsqrt(jnp.sum(value * value, -1, keepdims=True) + NORM_EPS)
                if part == 0:
                    scale = scale * head_dim ** (-0.5)
                value = value * scale
            parts[part].append(value)
        gates.append(sigmoid(logit_ref[:, head : head + 1]))
        column = slice(head * head_dim, (head + 1) * head_dim)
        recall = recall_ref[:, column]
        pulled = mixed_grad_ref[:, column] * valid
        scale = lax.rsqrt(jnp.mean(recall * recall, -1, keepdims=True) + HEAD_EPS)
        normed = recall * scale
        gain_grad = gain_grad + jnp.sum(pulled * normed, 0, keepdims=True)
        pulled = pulled * gain
        recall_grads.append(
            scale * (pulled - normed * jnp.mean(normed * pulled, -1, keepdims=True))
        )
    gain_grad_ref[...] += gain_grad
    strengths = [gate * valid for gate in gates]
    same, strict, lower, eye = block_masks(stacked)
    query_grads = [None] * blocks
    key_grads = [None] * blocks
    value_grads = [None] * blocks
    strength_grads = [None] * blocks
    for index in range(blocks - 1, -1, -1):
        queries = stack_heads(parts[0], index).astype(BF16)
        keys = stack_heads(parts[1], index).astype(BF16)
        values = stack_heads(parts[2], index)
        strength = stack_heads(strengths, index)
        out_grad = stack_heads(recall_grads, index).astype(BF16)
        inverse = inverse_ref[index]
        weighted = weight_ref[index]
        update = update_ref[index]
        gram = low_dot(keys, keys, 1, 1)
        scores = jnp.where(lower, low_dot(queries, keys, 1, 1), 0.0).astype(BF16)
        local_grad = low_dot(scores, out_grad, 0, 0)
        score_grad = jnp.where(lower, low_dot(out_grad, update, 1, 1), 0.0).astype(BF16)
        keep = (pos[index * BLOCK : index * BLOCK + 1] != 0).astype(F32)
        update_grads = []
        query_carried = []
        key_carried = []
        misses = []
        starts = []
        for head in range(heads):
            span = slice(head * BLOCK, (head + 1) * BLOCK)
            ahead = state_ref[head]
            ahead_low = ahead.astype(BF16)
            start = start_ref[index, head]
            starts.append(start)
            update_grad = local_grad[span] + low_dot(keys[span], ahead_low, 1, 1)
            update_grad_low = update_grad.astype(BF16)
            update_grads.append(update_grad_low)
            carried = ahead + low_dot(out_grad[span], queries[span], 0, 0)
            carried = carried - low_dot(update_grad_low, weighted[span], 0, 0)
            state_ref[head] = carried * keep
            query_carried.append(low_dot(out_grad[span], start, 1, 0))
            key_carried.append(low_dot(update[span], ahead_low, 1, 0))
            misses.append(values[span] - low_dot(keys[span], start, 1, 1))
        miss_grad = low_dot(inverse, jnp.concatenate(update_grads, axis=0), 0, 0)
        miss = jnp.concatenate(misses, axis=0)
        system_grad = jnp.where(strict, -low_dot(miss_grad, update, 1, 1), 0.0)
        strength_grads[index] = jnp.sum(miss_grad * miss, -1, keepdims=True) + jnp.sum(
            system_grad * gram, -1, keepdims=True
        )
        gram_grad = (strength * system_grad).astype(BF16)
        value_grad = strength * miss_grad
        value_low = value_grad.astype(BF16)
        value_grads[index] = value_grad
        query_grads[index] = jnp.concatenate(query_carried, axis=0) + low_dot(score_grad, keys, 1, 0)
        key_grad = jnp.concatenate(key_carried, axis=0) + low_dot(score_grad, queries, 0, 0)
        key_grad = key_grad + low_dot(gram_grad, keys, 1, 0) + low_dot(gram_grad, keys, 0, 0)
        key_state = [
            low_dot(value_low[head * BLOCK : (head + 1) * BLOCK], starts[head], 1, 0)
            for head in range(heads)
        ]
        key_grads[index] = key_grad - jnp.concatenate(key_state, axis=0)
    grads = [query_grads, key_grads, value_grads]
    logit_grads = []
    for head in range(heads):
        span = slice(head * BLOCK, (head + 1) * BLOCK)
        gate = gates[head]
        pulled = jnp.concatenate([strength_grads[index][span] for index in range(blocks)], axis=0)
        logit_grads.append(pulled * valid * gate * (1.0 - gate))
        for part in range(3):
            pulled = jnp.concatenate([grads[part][index][span] for index in range(blocks)], axis=0)
            total, shifted, taps = conv_part(
                proj_ref, before_ref, conv_ref, reach, part, head, head_dim, heads
            )
            gate_part = sigmoid(total)
            value = total * gate_part
            if part < 2:
                scale = lax.rsqrt(jnp.sum(value * value, -1, keepdims=True) + NORM_EPS)
                normed = value * scale
                pulled = scale * (pulled - normed * jnp.sum(normed * pulled, -1, keepdims=True))
                if part == 0:
                    pulled = pulled * head_dim ** (-0.5)
            pre_grad = pulled * gate_part * (1.0 + total * (1.0 - gate_part))
            column = slice(part * width + head * head_dim, part * width + (head + 1) * head_dim)
            tap_column = slice(head * head_dim, (head + 1) * head_dim)
            for lag in range(4):
                conv_grad_ref[part * 4 + lag : part * 4 + lag + 1, tap_column] += jnp.sum(
                    pre_grad * shifted[lag], 0, keepdims=True
                )
            joined = jnp.concatenate([pre_grad, halo_ref[:, column]], axis=0)
            total_grad = taps[0] * pre_grad
            for lag in range(1, 4):
                total_grad = total_grad + taps[lag] * (joined * reach_ahead[lag])[lag : lag + rows]
            proj_grad_ref[:, column] = total_grad.astype(BF16)
            halo_ref[:, column] = pre_grad[:HALO]
    blank = jnp.zeros((rows, LANES - heads), F32)
    proj_grad_ref[:, 3 * width :] = jnp.concatenate(logit_grads + [blank], axis=1).astype(BF16)


def mixer_specs(rows, columns, order):
    blocks = rows // BLOCK
    ratio = rows // HALO

    def whole(*shape):
        return pl.BlockSpec(shape, lambda step: (0,) * len(shape))

    def by_rows(size, column=0):
        return pl.BlockSpec((rows, size), lambda step: (order(step), column))

    def by_blocks(*tail):
        return pl.BlockSpec((blocks,) + tail, lambda step: (order(step),) + (0,) * len(tail))

    before = pl.BlockSpec(
        (HALO, columns), lambda step: (jnp.maximum(order(step) * ratio - 1, 0), 0)
    )
    return whole, by_rows, by_blocks, before


def mixer_forward(projected, conv_rows, head_gain, pos, valid, heads):
    slots = projected.shape[0]
    head_dim = head_gain.shape[1]
    width = heads * head_dim
    columns = 3 * width
    rows = slots // lax.axis_size("tensor")
    steps = slots // rows
    stacked = heads * BLOCK
    block_count = slots // BLOCK
    whole, by_rows, by_blocks, before = mixer_specs(rows, columns, lambda step: step)
    return pl.pallas_call(
        lambda *refs: forward_kernel(*refs, heads=heads, head_dim=head_dim),
        grid=(steps,),
        in_specs=[
            by_rows(columns),
            before,
            by_rows(LANES, columns // LANES),
            by_rows(1),
            by_rows(1),
            whole(12, width),
            whole(1, head_dim),
        ],
        out_specs=[
            by_rows(width),
            by_rows(width),
            by_blocks(heads, head_dim, head_dim),
            by_blocks(stacked, stacked),
            by_blocks(stacked, head_dim),
            by_blocks(stacked, head_dim),
        ],
        scratch_shapes=[pltpu.VMEM((heads, head_dim, head_dim), F32)],
        out_shape=[
            jax.ShapeDtypeStruct((slots, width), BF16),
            jax.ShapeDtypeStruct((slots, width), F32),
            jax.ShapeDtypeStruct((block_count, heads, head_dim, head_dim), BF16),
            jax.ShapeDtypeStruct((block_count, stacked, stacked), BF16),
            jax.ShapeDtypeStruct((block_count, stacked, head_dim), BF16),
            jax.ShapeDtypeStruct((block_count, stacked, head_dim), BF16),
        ],
        name="mixer_forward",
    )(projected, projected, projected, pos, valid, conv_rows, head_gain)


def mixer_backward(projected, conv_rows, head_gain, pos, valid, heads, kept, mixed_grad):
    slots = projected.shape[0]
    head_dim = head_gain.shape[1]
    width = heads * head_dim
    columns = 3 * width
    rows = slots // lax.axis_size("tensor")
    steps = slots // rows
    stacked = heads * BLOCK
    ratio = rows // HALO
    recall, start, inverse, update, weighted = kept
    pos_padded = jnp.pad(pos, ((0, HALO), (0, 0)))
    whole, by_rows, by_blocks, before = mixer_specs(rows, columns, lambda step: steps - 1 - step)
    return pl.pallas_call(
        lambda *refs: backward_kernel(*refs, heads=heads, head_dim=head_dim),
        grid=(steps,),
        in_specs=[
            by_rows(columns),
            before,
            by_rows(LANES, columns // LANES),
            by_rows(1),
            pl.BlockSpec((HALO, 1), lambda step: ((steps - step) * ratio, 0)),
            by_rows(1),
            whole(12, width),
            whole(1, head_dim),
            by_rows(width),
            by_blocks(heads, head_dim, head_dim),
            by_blocks(stacked, stacked),
            by_blocks(stacked, head_dim),
            by_blocks(stacked, head_dim),
            by_rows(width),
        ],
        out_specs=[by_rows(columns + LANES), whole(12, width), whole(1, head_dim)],
        scratch_shapes=[
            pltpu.VMEM((heads, head_dim, head_dim), F32),
            pltpu.VMEM((HALO, columns), F32),
        ],
        out_shape=[
            jax.ShapeDtypeStruct((slots, columns + LANES), BF16),
            jax.ShapeDtypeStruct((12, width), F32),
            jax.ShapeDtypeStruct((1, head_dim), F32),
        ],
        name="mixer_backward",
    )(
        projected, projected, projected, pos, pos_padded, valid, conv_rows, head_gain,
        recall, start, inverse, update, weighted, mixed_grad,
    )


def doc_layout(length_pair, slot_count):
    first_end = (length_pair[0] + BLOCK - 1) // BLOCK * BLOCK
    second_end = first_end + (length_pair[1] + BLOCK - 1) // BLOCK * BLOCK
    places = jnp.arange(slot_count, dtype=jnp.int32)
    in_first = places < first_end
    in_second = jnp.logical_and(places >= first_end, places < second_end)
    doc_begin = jnp.where(in_first, 0, jnp.where(in_second, first_end, second_end))
    doc_limit = jnp.where(in_first, length_pair[0], jnp.where(in_second, length_pair[1], 0))
    offset = places - doc_begin
    is_valid = (offset < doc_limit).astype(F32)
    return offset.astype(F32)[:, None], is_valid[:, None]


def ring_shift(value, step):
    size = lax.axis_size("tensor")
    return lax.ppermute(value, "tensor", [(place, (place + step) % size) for place in range(size)])


def held(value, *others):
    return lax.optimization_barrier((value, others))[0]


def piece_start(step, count):
    size = lax.axis_size("tensor")
    return lax.rem(lax.axis_index("tensor") + step, size) * count


def gather_rows(rows, *token, mid=()):
    size = lax.axis_size("tensor")
    count = rows.shape[0]
    half = count // 2
    rows = held(rows, token)
    full = jnp.zeros((size * count, rows.shape[1]), rows.dtype)

    def put(full, piece, step, at=0):
        return lax.dynamic_update_slice(full, piece, (piece_start(step, count) + at, 0))

    full = put(full, rows, 0)
    from_left = rows
    from_right = rows
    for step in range(1, size // 2):
        from_left = ring_shift(from_left, 1)
        from_right = ring_shift(from_right, -1)
        full = put(full, from_left, size - step)
        full = put(full, from_right, step)
    from_left_half, from_right_half = from_left[:half], from_right[half:]
    if mid:
        from_left_half, from_right_half = held((from_left_half, from_right_half), mid)
    far = ring_shift(from_left_half, 1), ring_shift(from_right_half, -1)
    full = put(full, far[0], size // 2)
    full = put(full, far[1], size // 2, half)
    return full, (from_left, from_right), far


def ring_rows(low, step, at, length):
    count = low.shape[0] // lax.axis_size("tensor")
    start = piece_start(step, count) + at
    return lax.dynamic_slice(low, (start, 0), (length, low.shape[1])).astype(F32)


def scatter_rows_begin(partial, *token):
    size = lax.axis_size("tensor")
    half = partial.shape[0] // size // 2
    low = held(partial, token)
    to_right = ring_shift(ring_rows(low, size // 2, 0, half).astype(BF16), 1)
    to_left = ring_shift(ring_rows(low, size // 2, half, half).astype(BF16), -1)
    return low, (to_right, to_left)


def scatter_rows_end(state, *token):
    size = lax.axis_size("tensor")
    low, (to_right, to_left) = state
    count = low.shape[0] // size
    half = count // 2
    if token:
        to_right, to_left = held((to_right, to_left), token)
    for step in range(size // 2 - 1, 0, -1):
        right = ring_rows(low, step, 0, count)
        left = ring_rows(low, size - step, 0, count)
        if step == size // 2 - 1:
            right = joined([right[:half] + to_right.astype(F32), right[half:]])
            left = joined([left[:half], left[half:] + to_left.astype(F32)])
        else:
            right = right + to_right.astype(F32)
            left = left + to_left.astype(F32)
        to_right = ring_shift(right.astype(BF16), 1)
        to_left = ring_shift(left.astype(BF16), -1)
    total = ring_rows(low, 0, 0, count) + to_right.astype(F32) + to_left.astype(F32)
    return total, (to_right, to_left)


def scatter_rows(partial, *token, mid=()):
    state = scatter_rows_begin(partial, *token)
    total, last = scatter_rows_end(state, *mid)
    return total, state[1], last


def dot(left, right, left_dim, right_dim, out_type=F32):
    return lax.dot_general(
        left, right, (((left_dim,), (right_dim,)), ((), ())), preferred_element_type=out_type
    )


def gather_dp(value):
    return lax.all_gather(value, "dp", axis=0, tiled=True)


def scatter_dp(value):
    return lax.psum_scatter(value, "dp", scatter_dimension=0, tiled=True)


def row_scale(values):
    return lax.rsqrt(jnp.mean(values * values, -1, keepdims=True) + NORM_EPS)


def norm_pull(values, pulled):
    scale = row_scale(values)
    normed = values * scale
    return scale * (pulled - normed * jnp.mean(normed * pulled, -1, keepdims=True))


def joined(parts):
    return jnp.concatenate(parts, axis=0)


def per_device(
    tokens, cotangent, doc_lengths, attn_gain, w_qkv, w_beta, conv_weight, head_gain,
    w_out, ffn_gain, w_gate_up, w_down,
):
    batches, local_rows, width = tokens.shape
    size = lax.axis_size("tensor")
    dp_size = lax.axis_size("dp")
    slots = local_rows * size
    shard = w_qkv.shape[0]
    heads = w_beta.shape[1]
    units = w_down.shape[0]
    head_share = head_gain.shape[0]
    head_dim = head_share * dp_size
    columns = 3 * heads * head_dim
    conv_share = 12 * heads * head_share
    small_share = conv_share + head_share
    extra = -(-small_share // shard)
    small_at = columns + heads

    attn_column = attn_gain.astype(F32)[:, None]
    ffn_column = ffn_gain.astype(F32)[:, None]
    qkv_rows = jnp.concatenate([w_qkv.reshape(shard, columns), w_beta], axis=1).astype(F32)
    small = jnp.concatenate(
        [conv_weight.reshape(-1), head_gain, jnp.zeros((extra * shard - small_share,), BF16)]
    ).reshape(shard, extra)
    blank = jnp.zeros((shard, LANES - heads - extra), BF16)
    full_proj = gather_dp(
        jnp.concatenate([(attn_column * qkv_rows).astype(BF16), small, blank], axis=1)
    )
    full_out = gather_dp(w_out.T)
    gate_up_rows = w_gate_up.reshape(shard, 2 * units).astype(F32)
    full_gate_up = gather_dp((ffn_column * gate_up_rows).astype(BF16))
    full_down = gather_dp(w_down.T)
    small = full_proj[:, small_at : small_at + extra].astype(F32).reshape(dp_size, extra * shard)
    full_conv = small[:, :conv_share].reshape(dp_size, 12, heads, head_share)
    full_conv = jnp.transpose(full_conv, (1, 2, 0, 3)).reshape(12, heads * head_dim)
    full_head_gain = small[:, conv_share:small_share].reshape(1, head_dim)

    rows = [tokens[index].astype(F32) for index in range(batches)]
    layouts = [doc_layout(doc_lengths[index, 0], slots) for index in range(batches)]

    def mix(index, projected, *beside):
        mixed, *kept = mixer_forward(
            projected, full_conv, full_head_gain, *layouts[index], heads
        )
        return mixed, kept, dot(held(mixed, beside), full_out, 1, 1, BF16)

    def after_mixer(index, branch):
        hidden = rows[index] + branch
        return hidden, (hidden * row_scale(hidden)).astype(BF16)

    def feed(ffn_full):
        gate_up = dot(ffn_full, full_gate_up, 1, 0)
        gate = gate_up[:, :units]
        activated = (gate * sigmoid(gate) * gate_up[:, units:]).astype(BF16)
        return gate_up, activated

    def feed_back(gate_up, cot_full, *beside):
        grad_act = dot(cot_full, full_down, 1, 0)
        gate = gate_up[:, :units]
        up = gate_up[:, units:]
        opened = sigmoid(gate)
        grad_gate = grad_act * up * opened * (1.0 + gate * (1.0 - opened))
        grad_up = grad_act * (gate * opened)
        grad_gate_up = jnp.concatenate([grad_gate, grad_up], axis=1).astype(BF16)
        return grad_gate_up, dot(held(grad_gate_up, beside), full_gate_up, 1, 1, BF16)

    def before_ffn(index, hidden, pulled):
        return cotangent[index].astype(F32) + norm_pull(hidden, pulled)

    attn_in = [(rows[index] * row_scale(rows[index])).astype(BF16) for index in range(batches)]
    attn_0, first, last = gather_rows(attn_in[0])
    attn_1, attn_first, _ = gather_rows(attn_in[1], last, full_proj)
    cot_0, cot_first, _ = gather_rows(cotangent[0], last, full_proj)
    proj_0 = dot(attn_0, full_proj, 1, 0)
    mixed_0, kept_0, part_0 = mix(0, proj_0, attn_first, cot_first)

    branch, first, last = scatter_rows(part_0)
    proj_1 = dot(attn_1, full_proj, 1, 0)
    mixed_1, kept_1, part_1 = mix(1, held(proj_1, first), last, cot_0)
    hidden_0, ffn_in = after_mixer(0, branch)

    ffn_0, ffn_first, _ = gather_rows(ffn_in, part_1, full_gate_up)
    branch, first, last = scatter_rows(part_1, ffn_first)
    gate_up_0, act_0 = feed(held(ffn_0, first))
    grad_gate_up_0, part_0 = feed_back(gate_up_0, cot_0, last)
    cot_1 = lax.all_gather(held(cotangent[1], gate_up_0), "tensor", axis=0, tiled=True)
    hidden_1, ffn_in = after_mixer(1, branch)

    ffn_1, ffn_first, _ = gather_rows(ffn_in)
    down_0 = dot(held(act_0, part_0), full_down, 1, 1, BF16)
    down_grad = dot(held(cot_0, down_0), act_0, 0, 0, BF16)
    pulled, first, last = scatter_rows(part_0, ffn_first)
    gate_up_grad = dot(held(ffn_0, down_grad, ffn_first), grad_gate_up_0, 0, 0, BF16)
    gate_up_1, act_1 = feed(held(ffn_1, first, gate_up_grad))
    down_state = scatter_rows_begin(down_0, first)
    grad_gate_up_1, part_1 = feed_back(gate_up_1, cot_1, last, down_state[1])
    grad_hidden_0 = before_ffn(0, hidden_0, pulled)

    branch_0, first, last = gather_rows(grad_hidden_0.astype(BF16))
    down_grad = (down_grad + dot(held(cot_1, part_1, first), act_1, 0, 0)).astype(BF16)
    pulled, first, last = scatter_rows(part_1, first)
    gate_up_grad = gate_up_grad + dot(held(ffn_1, first, branch_0, down_grad), grad_gate_up_1, 0, 0)
    gate_up_grad = gate_up_grad.astype(BF16)
    grad_hidden_1 = before_ffn(1, hidden_1, pulled)

    branch_in = held(grad_hidden_1.astype(BF16), gate_up_grad)
    branch_1, branch_first, _ = gather_rows(branch_in)
    down_grad = scatter_dp(down_grad)
    gate_up_grad = scatter_dp(gate_up_grad)
    down_1 = dot(held(act_1, branch_in), full_down, 1, 1, BF16)
    grad_mixed = dot(held(branch_0, branch_in), full_out, 1, 0)
    grad_mixed = held(grad_mixed, branch_first, down_1)
    grad_proj_0, conv_grad_0, gain_grad_0 = mixer_backward(
        proj_0, full_conv, full_head_gain, *layouts[0], heads, kept_0, grad_mixed
    )
    lower_0, down_last = scatter_rows_end(down_state, branch_first)
    part_0 = dot(held(grad_proj_0, branch_1, down_last), full_proj, 1, 1, BF16)

    pulled, first, last = scatter_rows(part_0)
    out_grad = dot(
        joined([held(branch_0, part_0), branch_1]), joined([mixed_0, mixed_1]), 0, 0, BF16
    )
    grad_mixed = dot(held(branch_1, part_0), full_out, 1, 0)
    input_rows_0 = grad_hidden_0 + norm_pull(rows[0], pulled)
    grad_mixed = held(grad_mixed, first, out_grad)
    out_grad = scatter_dp(out_grad)
    grad_proj_1, conv_grad_1, gain_grad_1 = mixer_backward(
        proj_1, full_conv, full_head_gain, *layouts[1], heads, kept_1, grad_mixed
    )
    part_1 = dot(held(grad_proj_1, last), full_proj, 1, 1, BF16)
    attn_all = joined([held(attn_0, last), attn_1])
    pulled, first, last = scatter_rows(part_1, last, down_grad, gate_up_grad)
    down_out = down_grad.T.astype(F32)
    proj_grad = dot(attn_all, joined([grad_proj_0, grad_proj_1]), 0, 0, BF16)
    conv_grad = (conv_grad_0 + conv_grad_1).reshape(12, heads, dp_size, head_share)
    conv_grad = jnp.transpose(conv_grad, (2, 0, 1, 3)).reshape(dp_size, conv_share)
    head_gain_grad = (gain_grad_0 + gain_grad_1).reshape(dp_size, head_share)
    small_grad = jnp.concatenate(
        [conv_grad, head_gain_grad, jnp.zeros((dp_size, extra * shard - small_share), F32)], axis=1
    )
    small_grad = small_grad.reshape(dp_size * shard, extra).astype(BF16)
    small_grad = jnp.pad(small_grad, ((0, 0), (small_at, LANES - heads - extra)))
    proj_grad = scatter_dp(proj_grad + small_grad)
    gate_up_grad = gate_up_grad.astype(F32)
    gate_up_out = (gate_up_grad * ffn_column).reshape(shard, 2, units)
    ffn_gain_grad = jnp.sum(gate_up_grad * gate_up_rows, axis=1)
    out_out = out_grad.T.astype(F32)
    lower_1, first, last = scatter_rows(
        down_1, last, down_out, mid=(gate_up_out, ffn_gain_grad, out_out)
    )
    proj_grad = held(proj_grad, first)
    input_rows_1 = grad_hidden_1 + norm_pull(rows[1], pulled)
    layer_rows_0 = (hidden_0 + lower_0).astype(BF16)
    layer_rows_1 = (hidden_1 + lower_1).astype(BF16)

    proj_grad = proj_grad.astype(F32)
    small_grad = proj_grad[:, small_at : small_at + extra].reshape(extra * shard)
    gain_grads = jnp.concatenate(
        [
            jnp.sum(proj_grad[:, :small_at] * qkv_rows, axis=1),
            ffn_gain_grad,
            small_grad[conv_share:small_share],
        ]
    )[None]
    gain_grads = held(gain_grads, last)
    total = gain_grads
    for step in range(1, size):
        total = total + ring_shift(gain_grads, step)
    total = total[0]
    proj_grad = proj_grad[:, :small_at] * attn_column
    return (
        jnp.stack([layer_rows_0, layer_rows_1]),
        jnp.stack([input_rows_0, input_rows_1]),
        total[:shard],
        proj_grad[:, :columns].reshape(shard, 3, -1),
        proj_grad[:, columns:],
        small_grad[:conv_share].reshape(3, 4, heads, head_share),
        total[2 * shard :],
        out_out,
        total[shard : 2 * shard],
        gate_up_out,
        down_out,
    )


def solution(mesh):
    return jax.shard_map(
        per_device,
        mesh=mesh,
        in_specs=(
            P(None, ("dp", "tensor"), None),
            P(None, ("dp", "tensor"), None),
            P(None, "dp", None),
            P("dp"),
            P("dp", None, "tensor"),
            P("dp", "tensor"),
            P(None, None, "tensor", "dp"),
            P("dp"),
            P("tensor", "dp"),
            P("dp"),
            P("dp", None, "tensor"),
            P("tensor", "dp"),
        ),
        out_specs=(
            P(None, ("dp", "tensor"), None),
            P(None, ("dp", "tensor"), None),
            P("dp"),
            P("dp", None, "tensor"),
            P("dp", "tensor"),
            P(None, None, "tensor", "dp"),
            P("dp"),
            P("tensor", "dp"),
            P("dp"),
            P("dp", None, "tensor"),
            P("tensor", "dp"),
        ),
        check_vma=False,
    )
```
